256 devices in a mesh: gx: 32 (over y, z_hi, x), gy: 8 (over z_lo, core).
Axes of the slice: x: 4, y: 4, z: 8 (z_hi: 2, z_lo: 4; z = z_hi * 4 + z_lo), core: 2. Of those that a mesh axis runs over, the one named last changes fastest.
Arguments:
- fluid_position: float32 [3, 32, 8, 4096], P(None, 'gx', 'gy'), may hold values from 0 to 1
- fluid_velocity: float32 [3, 32, 8, 4096], P(None, 'gx', 'gy'), may hold values from -6 to 6
- fluid_mass: float32 [32, 8, 4096], P('gx', 'gy'), may hold values from 0.5 to 2
- fluid_counts: int32 [32, 8, 32], P('gx', 'gy'), may hold values from 1 to 128
- fluid_lists: int32 [32, 8, 32, 8], P('gx', 'gy'), may hold values from 0 to 287, as said below
- coupling_lists: int32 [32, 8, 32, 4], P('gx', 'gy'), may hold values from 0 to 143
- boulder_position: float32 [3, 32, 8, 2048], P(None, 'gx', 'gy'), may hold values from 0 to 1, as said below
- boulder_velocity: float32 [3, 32, 8, 2048], P(None, 'gx', 'gy'), may hold values from -6 to 6
- boulder_radius: float32 [32, 8, 2048], P('gx', 'gy'), may hold values from 0.03 to 0.07
- boulder_mass: float32 [32, 8, 2048], P('gx', 'gy'), may hold values from 0.5 to 2
- boulder_counts: int32 [32, 8, 16], P('gx', 'gy'), may hold values from 1 to 128
- contact_ids: int32 [32, 8, 8, 2048], P('gx', 'gy'), may hold values from 0 to 18431, as said below
- spring_history: float32 [3, 32, 8, 8, 2048], P(None, 'gx', 'gy'), may hold values from -0.3 to 0.3
Outputs:
- fluid_accel: float32 [3, 32, 8, 4096], P(None, 'gx', 'gy')
- fluid_density: float32 [32, 8, 4096], P('gx', 'gy')
- boulder_accel: float32 [3, 32, 8, 2048], P(None, 'gx', 'gy')
- history_out: float32 [3, 32, 8, 8, 2048], P(None, 'gx', 'gy')
The draws below stay inside these ranges and needn't reach their ends.
Inputs may be any that keep to these rules, and one draw needn't show every extreme that they name: `fluid_lists`: entry n names block n % 32 of the tile offset by n // 96 - 1 along gx and n // 32 % 3 - 1 along gy, periodically; never the listing block itself; repeats may occur. `coupling_lists`: entry n names boulder block n % 16 of the tile offset by n // 48 - 1 along gx and n // 16 % 3 - 1 along gy, periodically; repeats may occur. `contact_ids`: entry n names boulder n % 2048 of the tile offset by n // 6144 - 1 along gx and n // 2048 % 3 - 1 along gy, periodically; partners are nearby boulders of the same or an adjacent tile; never the boulder itself; partners may be dead slots. `boulder_position`: x and y lie in [0, 1); z is nonnegative.
All inputs are finite; a program needn't handle non-finite values.
Results may differ from the reference program's by a relative error of at most 0.0003.
Values sent between devices are 32-bit elements; how exact they have to be, the bound alone decides.
A program may use at most 64 MiB of HBM per device.

```python
import math
import jax
import jax.numpy as jnp
from jax import lax

BLOCK = 128
FB = 32
BB = 16
K = 8
KC = 4
S = 8
NF_DEV = 4096
NB_DEV = 2048
N_GX = 32
N_GY = 8


def draw_fluid_lists(key, part):
    drawn = jax.random.randint(key, (N_GX, N_GY, FB, K), 0, 9 * FB - 1, dtype=jnp.int32)
    itself = 4 * FB + jnp.arange(FB, dtype=jnp.int32)[None, None, :, None]
    return drawn + (drawn >= itself).astype(jnp.int32)


def tile_permutation(tile_key):
    return jax.random.permutation(tile_key, NB_DEV).astype(jnp.int32)


def lattice_sites(key):
    tile_keys = jax.random.split(jax.random.fold_in(key, 7), N_GX * N_GY)
    sites = jax.vmap(tile_permutation)(tile_keys)
    return sites.reshape(N_GX, N_GY, NB_DEV)


def draw_boulder_position(key, part):
    sites = lattice_sites(key)
    layer = sites // 128
    within = sites % 128
    column_x = within // 8
    column_y = within % 8
    centre = jnp.stack([(column_x.astype(jnp.float32) + 0.5) / 16.0, (column_y.astype(jnp.float32) + 0.5) / 8.0, (layer.astype(jnp.float32) + 0.5) / 16.0])
    jitter = jax.random.uniform(jax.random.fold_in(key, 11), (3, N_GX, N_GY, NB_DEV), jnp.float32, -0.01, 0.01)
    return centre + jitter


def draw_contact_ids(key, part):
    sites = lattice_sites(key)
    slot_of_site = jnp.argsort(sites, axis=-1).astype(jnp.int32)
    layer = (sites // 128)[:, :, None, :]
    within = sites % 128
    column_x = (within // 8)[:, :, None, :]
    column_y = (within % 8)[:, :, None, :]
    offset_x = jnp.array([1, -1, 0, 0, 0, 0, 1, -1], dtype=jnp.int32)[:S][None, None, :, None]
    offset_y = jnp.array([0, 0, 1, -1, 0, 0, 0, 0], dtype=jnp.int32)[:S][None, None, :, None]
    offset_z = jnp.array([0, 0, 0, 0, 1, -1, 1, -1], dtype=jnp.int32)[:S][None, None, :, None]
    moved_x = column_x + offset_x
    moved_y = column_y + offset_y
    tile_x = (moved_x + 16) // 16 - 1
    tile_y = (moved_y + 8) // 8 - 1
    partner_site = (layer + offset_z + BB) % BB * 128 + moved_x % 16 * 8 + moved_y % 8
    home_x = jnp.arange(N_GX, dtype=jnp.int32)[:, None, None, None]
    home_y = jnp.arange(N_GY, dtype=jnp.int32)[None, :, None, None]
    other_x = (home_x + tile_x + N_GX) % N_GX
    other_y = (home_y + tile_y + N_GY) % N_GY
    partner_slot = slot_of_site[other_x, other_y, partner_site]
    entry = ((tile_x + 1) * 3 + (tile_y + 1)) * NB_DEV + partner_slot
    scores = jax.random.randint(jax.random.fold_in(key, 23), (N_GX, N_GY, S, NB_DEV), 0, 1000, dtype=jnp.int32) * S + jnp.arange(S, dtype=jnp.int32)[None, None, :, None]
    order = jnp.argsort(scores, axis=2, stable=True).astype(jnp.int32)
    return jnp.take_along_axis(entry, order, axis=2)


def place_ends(values, own_key, least, high):
    shape = values.shape
    place = [jax.random.randint(jax.random.fold_in(own_key, axis), (), 0, shape[axis]) for axis in range(len(shape))]
    values = values.at[tuple(place)].set(least)
    longest = shape.index(max(shape))
    place[longest] = (place[longest] + 1) % shape[longest]
    return values.at[tuple(place)].set(high)


def level_of(key, dims, cuts, low, top_value):
    def one(dim, blocks):
        steps = jax.random.uniform(jax.random.fold_in(jax.random.fold_in(key, 6), dim), (blocks,), jnp.float32, low / len(cuts), top_value / len(cuts))
        return jnp.repeat(jnp.exp(steps), dims[dim] // blocks).reshape((-1,) + (1,) * (len(dims) - dim - 1))

    level = one(*cuts[0])
    for cut in cuts[1:]:
        level = level * one(*cut)
    return level


def noise(stream_key, dims, scale, bound, shards=(), kind=jnp.bfloat16):
    gain = level_of(stream_key, dims, shards, -0.22, 0.18) if shards else 1.0
    result = jax.random.normal(stream_key, dims, jnp.float32) * scale * gain
    return jnp.minimum(jnp.maximum(result, -bound), bound).astype(kind)


def setup_inputs(seed: int = 0) -> dict:
    arg_keys = jax.random.split(jax.random.key(seed), 14)
    return {
        "fluid_position": jnp.clip(1.0 * jax.random.uniform(arg_keys[0], (3, N_GX, N_GY, NF_DEV), jnp.float32) ** level_of(arg_keys[0], (3, N_GX, N_GY, NF_DEV), ((1, 32), (2, 8)), -0.2, 0.2), 0.0, 1.0),
        "fluid_velocity": noise(arg_keys[1], (3, N_GX, N_GY, NF_DEV), 1.0, 6.0, ((1, 32), (2, 8)), jnp.float32),
        "fluid_mass": jnp.clip(jnp.exp(math.log(2.0) - 1.3862944 * jax.random.uniform(arg_keys[2], (N_GX, N_GY, NF_DEV), jnp.float32) ** level_of(arg_keys[2], (N_GX, N_GY, NF_DEV), ((0, 32), (1, 8)), -0.2, 0.2)), 0.5, 2.0),
        "fluid_counts": place_ends(jax.random.randint(arg_keys[3], (N_GX, N_GY, FB), 1, BLOCK + 1), jax.random.fold_in(arg_keys[3], 1), 1, BLOCK).astype(jnp.int32),
        "fluid_lists": draw_fluid_lists(jax.random.fold_in(arg_keys[13], 71), 0),
        "coupling_lists": place_ends(jax.random.randint(arg_keys[5], (N_GX, N_GY, FB, KC), 0, 9 * BB), jax.random.fold_in(arg_keys[5], 1), 0, (9 * BB) - 1).astype(jnp.int32),
        "boulder_position": draw_boulder_position(jax.random.fold_in(arg_keys[13], 71), 0),
        "boulder_velocity": noise(arg_keys[7], (3, N_GX, N_GY, NB_DEV), 1.0, 6.0, ((1, 32), (2, 8)), jnp.float32),
        "boulder_radius": jnp.clip(jnp.exp(math.log(0.07) - 0.8472979 * jax.random.uniform(arg_keys[8], (N_GX, N_GY, NB_DEV), jnp.float32) ** level_of(arg_keys[8], (N_GX, N_GY, NB_DEV), ((0, 32), (1, 8)), -0.2, 0.2)), 0.03, 0.07),
        "boulder_mass": jnp.clip(jnp.exp(math.log(2.0) - 1.3862944 * jax.random.uniform(arg_keys[9], (N_GX, N_GY, NB_DEV), jnp.float32) ** level_of(arg_keys[9], (N_GX, N_GY, NB_DEV), ((0, 32), (1, 8)), -0.2, 0.2)), 0.5, 2.0),
        "boulder_counts": place_ends(jax.random.randint(arg_keys[10], (N_GX, N_GY, BB), 1, BLOCK + 1), jax.random.fold_in(arg_keys[10], 1), 1, BLOCK).astype(jnp.int32),
        "contact_ids": draw_contact_ids(jax.random.fold_in(arg_keys[13], 71), 0),
        "spring_history": noise(arg_keys[12], (3, N_GX, N_GY, S, NB_DEV), 0.05, 0.3, ((1, 32), (2, 8)), jnp.float32),
    }


fluid_reach = 0.3
rest_density = 10.0
stiffness = 10.0
drag_strength = 1.0
couple_reach = 0.1
normal_stiffness = 10.0
shear_stiffness = 20.0
time_step = 0.05
intersection_scale = 0.01
soften_length = 0.02
gravity = 1.0

def block_shift(block_ids, per_tile):
    region = block_ids // per_tile
    along_x = (region // 3 - 1).astype(jnp.float32)
    along_y = (region % 3 - 1).astype(jnp.float32)
    return jnp.stack([along_x, along_y, jnp.zeros_like(along_x)])

def down_vector():
    return jnp.array([0.0, 0.0, -gravity], dtype=jnp.float32)

def density_local(position, mass_raw, fluid_hood, block_lists):
    blocks = block_lists.shape[0]
    group_size = min(blocks, 8)
    nearby = fluid_hood.reshape(9, 4, blocks, BLOCK)
    own_groups = position.reshape(3, blocks // group_size, group_size, BLOCK).transpose(1, 0, 2, 3)
    list_groups = block_lists.reshape(blocks // group_size, group_size, -1)

    def one_group(operands):
        own_position, block_ids = operands
        picked = nearby[block_ids // blocks, :, block_ids % blocks]
        other_position = jnp.moveaxis(picked[:, :, :3], 2, 0) + block_shift(block_ids, blocks)[..., None]
        distance = own_position[:, :, None, :, None] - other_position[:, :, :, None, :]
        radius_ratio = lax.optimization_barrier(jnp.sum(distance * distance, axis=0)) / fluid_reach ** 2
        kernel = jnp.maximum(1.0 - radius_ratio, 0.0) ** 3
        return lax.optimization_barrier(jnp.sum(picked[:, :, 3][:, :, None, :] * kernel, axis=(1, 3)))
    summed = lax.map(one_group, (own_groups, list_groups))
    return mass_raw + summed.reshape(-1)

def pressure_local(position, density, fluid_hood, density_hood, block_lists):
    blocks = block_lists.shape[0]
    group_size = min(blocks, 8)
    nearby = fluid_hood.reshape(9, 4, blocks, BLOCK)
    near_density = density_hood.reshape(9, blocks, BLOCK)
    own_weight = stiffness * (density / rest_density - 1.0) / (density * density)
    own_groups = position.reshape(3, blocks // group_size, group_size, BLOCK).transpose(1, 0, 2, 3)
    weight_groups = own_weight.reshape(blocks // group_size, group_size, BLOCK)
    list_groups = block_lists.reshape(blocks // group_size, group_size, -1)

    def one_group(operands):
        own_position, own_term, block_ids = operands
        picked = nearby[block_ids // blocks, :, block_ids % blocks]
        other_density = near_density[block_ids // blocks, block_ids % blocks]
        other_term = stiffness * (other_density / rest_density - 1.0) / (other_density * other_density)
        other_position = jnp.moveaxis(picked[:, :, :3], 2, 0) + block_shift(block_ids, blocks)[..., None]
        distance = own_position[:, :, None, :, None] - other_position[:, :, :, None, :]
        radius_ratio = lax.optimization_barrier(jnp.sum(distance * distance, axis=0)) / fluid_reach ** 2
        falloff = jnp.maximum(1.0 - radius_ratio, 0.0) ** 2
        pair_weight = picked[:, :, 3][:, :, None, :] * (own_term[:, None, :, None] + other_term[:, :, None, :]) * falloff * (6.0 / fluid_reach ** 2)
        return lax.optimization_barrier(jnp.sum(pair_weight[None] * distance, axis=(2, 4)))
    pushed = lax.map(one_group, (own_groups, weight_groups, list_groups))
    return pushed.transpose(1, 0, 2, 3).reshape(3, -1)

def coupling_local(position, velocity, mass_live, boulder_hood, block_lists):
    blocks = block_lists.shape[0]
    group_size = min(blocks, 8)
    boulder_blocks = boulder_hood.shape[-1] // BLOCK
    nearby = boulder_hood.reshape(9, 9, boulder_blocks, BLOCK)
    own_state = jnp.concatenate([position, velocity, mass_live[None]], axis=0)
    own_groups = own_state.reshape(7, blocks // group_size, group_size, BLOCK).transpose(1, 0, 2, 3)
    list_groups = block_lists.reshape(blocks // group_size, group_size, -1)

    def one_group(operands):
        fluid_state, block_ids = operands
        picked = nearby[block_ids // boulder_blocks, :, block_ids % boulder_blocks]
        state = jnp.moveaxis(picked, 2, 0)
        other_position = state[:3] + block_shift(block_ids, boulder_blocks)[..., None]
        distance = other_position[:, :, :, None, :] - fluid_state[:3, :, None, :, None]
        squared = lax.optimization_barrier(jnp.sum(distance * distance, axis=0))
        reach = state[6] + couple_reach
        falloff = jnp.maximum(1.0 - squared / (reach * reach)[:, :, None, :], 0.0) ** 2
        strength = drag_strength * fluid_state[6][:, None, :, None] * state[7][:, :, None, :] * falloff
        drag = strength[None] * (state[3:6][:, :, :, None, :] - fluid_state[3:6][:, :, None, :, None])
        return (lax.optimization_barrier(jnp.sum(drag, axis=(2, 4))), -lax.optimization_barrier(jnp.sum(drag, axis=3)))
    on_fluid, on_boulder = lax.map(one_group, (own_groups, list_groups))
    fluid_drag = on_fluid.transpose(1, 0, 2, 3).reshape(3, -1)
    flat_ids = block_lists.reshape(-1)
    spread = on_boulder.transpose(1, 0, 2, 3, 4).reshape(3, -1, BLOCK)
    partial_value = jnp.zeros((3, 9 * boulder_blocks, BLOCK), spread.dtype).at[:, flat_ids].add(spread)
    return (fluid_drag, partial_value.reshape(3, 3, 3, -1))

def contact_local(boulder_state, mass_raw, boulder_hood, partner_ids, history, coupled):
    boulder_count = boulder_state.shape[-1]
    flat_hood = boulder_hood.reshape(9, 9, boulder_count)
    picked = jnp.moveaxis(flat_hood[partner_ids // boulder_count, :, partner_ids % boulder_count], 2, 0)
    other_position = picked[:3] + block_shift(partner_ids, boulder_count)
    apart = boulder_state[:3, None, :] - other_position
    distance = jnp.sqrt(lax.optimization_barrier(jnp.sum(apart * apart, axis=0)) + soften_length ** 2)
    normal = apart / distance
    intersection = jnp.maximum(boulder_state[6][None, :] + picked[6] - distance, 0.0) * picked[8]
    relative = boulder_state[3:6, None, :] - picked[3:6]
    along = lax.optimization_barrier(jnp.sum(relative * normal, axis=0))
    sliding = relative - along * normal
    contact = jnp.minimum(intersection / intersection_scale, 1.0)
    spring = (history + time_step * sliding) * contact
    pushed = lax.optimization_barrier(jnp.sum(normal_stiffness * intersection * normal - shear_stiffness * spring, axis=1))
    live = boulder_state[8]
    accel = live * ((pushed + coupled) / mass_raw + down_vector()[:, None])
    return (accel, spring * live)

def wrap_pad(array):
    return jnp.pad(array, ((0, 0), (1, 1), (1, 1), (0, 0)), mode='wrap')

def neighbourhood(padded, row_index, column_index):
    zero_index = jnp.zeros((), jnp.int32)
    window = lax.dynamic_slice(padded, (zero_index, row_index, column_index, zero_index), (padded.shape[0], 3, 3, padded.shape[3]))
    return window.transpose(1, 2, 0, 3)

def reference(fluid_position, fluid_velocity, fluid_mass, fluid_counts, fluid_lists, coupling_lists, boulder_position, boulder_velocity, boulder_radius, boulder_mass, boulder_counts, contact_ids, spring_history):
    fluid_live = (jnp.arange(BLOCK, dtype=jnp.int32)[None, None, None, :] < fluid_counts[..., None]).reshape(N_GX, N_GY, NF_DEV).astype(jnp.float32)
    boulder_live = (jnp.arange(BLOCK, dtype=jnp.int32)[None, None, None, :] < boulder_counts[..., None]).reshape(N_GX, N_GY, NB_DEV).astype(jnp.float32)
    fluid_pack = jnp.concatenate([fluid_position, (fluid_mass * fluid_live)[None]], axis=0)
    boulder_pack = jnp.concatenate([boulder_position, boulder_velocity, boulder_radius[None], (boulder_mass * boulder_live)[None], boulder_live[None]], axis=0)
    fluid_padded = wrap_pad(fluid_pack)
    boulder_padded = wrap_pad(boulder_pack)
    devices = jnp.arange(N_GX * N_GY, dtype=jnp.int32)

    def first_pass(device):
        row_index = device // N_GY
        column_index = device % N_GY
        fluid_hood = neighbourhood(fluid_padded, row_index, column_index)
        boulder_hood = neighbourhood(boulder_padded, row_index, column_index)
        position = fluid_position[:, row_index, column_index]
        density = density_local(position, fluid_mass[row_index, column_index], fluid_hood, fluid_lists[row_index, column_index])
        drag, partial_value = coupling_local(position, fluid_velocity[:, row_index, column_index], fluid_mass[row_index, column_index] * fluid_live[row_index, column_index], boulder_hood, coupling_lists[row_index, column_index])
        return (density, drag, partial_value)
    density, drag, partial_value = lax.map(first_pass, devices)
    density = density.reshape(N_GX, N_GY, NF_DEV)
    partial_value = partial_value.reshape(N_GX, N_GY, 3, 3, 3, NB_DEV)
    coupled = jnp.zeros((N_GX, N_GY, 3, NB_DEV), jnp.float32)
    for index_x in range(3):
        for index_y in range(3):
            coupled = coupled + jnp.roll(partial_value[:, :, :, index_x, index_y], (index_x - 1, index_y - 1), axis=(0, 1))
    density_padded = wrap_pad(density[None])

    def second_pass(device):
        row_index = device // N_GY
        column_index = device % N_GY
        fluid_hood = neighbourhood(fluid_padded, row_index, column_index)
        density_hood = neighbourhood(density_padded, row_index, column_index)[:, :, 0]
        position = fluid_position[:, row_index, column_index]
        pushed = pressure_local(position, density[row_index, column_index], fluid_hood, density_hood, fluid_lists[row_index, column_index])
        accel = fluid_live[row_index, column_index] * (pushed + drag[device] / fluid_mass[row_index, column_index] + down_vector()[:, None])
        boulder_hood = neighbourhood(boulder_padded, row_index, column_index)
        boulder_accel, spring = contact_local(boulder_pack[:, row_index, column_index], boulder_mass[row_index, column_index], boulder_hood, contact_ids[row_index, column_index], spring_history[:, row_index, column_index], coupled[row_index, column_index])
        return (accel, boulder_accel, spring)
    accel, boulder_accel, spring = lax.map(second_pass, devices)
    fluid_accel = accel.reshape(N_GX, N_GY, 3, NF_DEV).transpose(2, 0, 1, 3)
    boulder_out = boulder_accel.reshape(N_GX, N_GY, 3, NB_DEV).transpose(2, 0, 1, 3)
    history_out = spring.reshape(N_GX, N_GY, 3, S, NB_DEV).transpose(2, 0, 1, 3, 4)
    return (fluid_accel, density * fluid_live, boulder_out, history_out)
```

```python
import jax
import jax.numpy as jnp
from jax import lax
from jax.experimental import pallas as pl
from jax.experimental.pallas import tpu as pltpu
from jax.sharding import PartitionSpec as P

F32 = jnp.float32
BF16 = jnp.bfloat16
MESH = pl.DeviceIdType.MESH
NT = (((1,), (1,)), ((), ()))
NN = (((1,), (0,)), ((), ()))

INV_H2 = 1.0 / 0.3**2
REST = 10.0
STIFF = 10.0
COUPLE = 0.1
NORMAL_K = 10.0
SHEAR_K = 20.0
DT = 0.05
SOFT2 = 0.02**2
PRESS_C = 6.0 / 0.3**2


def rounded(x):
    return x.astype(BF16).astype(F32)


def split3(x):
    hi = rounded(x)
    rest = x - hi
    mid = rounded(rest)
    return hi, mid, rest - mid


def dot(a, b, dims):
    return lax.dot_general(a, b, dims, preferred_element_type=F32)


def left_stack(x):
    h, m, l = split3(x)
    return jnp.concatenate([h, h, m, m, h, l], axis=0)


def right_stack(x):
    h, m, l = split3(x)
    return jnp.concatenate([h, m, h, m, l, h], axis=0).astype(BF16)


def stack3(x):
    return jnp.concatenate(split3(x), axis=0).astype(BF16)


def sum3(x):
    return x[0:8] + x[8:16] + x[16:24]


def row8(x):
    return jnp.broadcast_to(x, (8, x.shape[-1]))


def halves(x):
    hi = x.astype(BF16)
    return hi, (x - hi.astype(F32)).astype(BF16)


def tile_offsets(tile):
    third = (tile * 11) >> 5
    return (third - 1).astype(F32), (tile - 3 * third - 1).astype(F32)


def kernel(
    fl, cl, fcnt, bcnt,
    fpos, fvel, fmass, clv, bpos, bvel, brad, bmass,
    o_fa, o_fd, hb, o_cp,
    hf, hd, ut, qh, ql, fx, fu, fi, sp, cp, ry, red, rx,
    cnf, cnb, dens, dr, pf, ssem, rsem,
    *, n_x, n_y,
):
    me_x = lax.axis_index("gx")
    me_y = lax.axis_index("gy")
    xp = (lax.rem(me_x + 1, n_x), me_y)
    xm = (lax.rem(me_x + n_x - 1, n_x), me_y)
    yp = (me_x, lax.rem(me_y + 1, n_y))
    ym = (me_x, lax.rem(me_y + n_y - 1, n_y))

    barrier = pltpu.get_barrier_semaphore()
    for dev in (xp, xm, yp, ym):
        pl.semaphore_signal(barrier, inc=1, device_id=dev, device_id_type=MESH)

    row = lax.broadcasted_iota(jnp.int32, (8, 128), 0)
    lane = lax.broadcasted_iota(jnp.int32, (32, 128), 1)

    for b in range(32):
        cnf[b : b + 1, :] = jnp.full((1, 128), fcnt[b], jnp.int32)
    for b in range(16):
        cnb[b : b + 1, :] = jnp.full((1, 128), bcnt[b], jnp.int32)
    f_on = lane < cnf[...]
    b_on = lane[:16] < cnb[...]
    croot = jnp.where(f_on, jnp.exp(jnp.log(fmass[...]) * (1.0 / 3.0)), 0.0)
    for b in range(32):
        s = slice(b, b + 1)
        hf[128 + b] = jnp.concatenate(
            [croot[s], fpos[0, s, :], fpos[1, s, :], fpos[2, s, :]], axis=0
        )
    bm_live = jnp.where(b_on, bmass[...], 0.0)
    for b in range(16):
        s = slice(b, b + 1)
        hb[64 + b] = jnp.concatenate(
            [bm_live[s]]
            + [bpos[d, s, :] for d in range(3)]
            + [bvel[d, s, :] for d in range(3)]
            + [brad[s, :]],
            axis=0,
        )

    def copy(src, dst, k, dev):
        return pltpu.make_async_remote_copy(
            src_ref=src, dst_ref=dst, send_sem=ssem.at[k], recv_sem=rsem.at[k],
            device_id=dev, device_id_type=MESH,
        )

    def halo(ref, width, base):
        at = lambda t: ref.at[pl.ds(t * width, width)]
        return {
            1: copy(at(4), at(1), base + 0, xp),
            7: copy(at(4), at(7), base + 1, xm),
            3: copy(at(4), at(3), base + 2, yp),
            5: copy(at(4), at(5), base + 3, ym),
            0: copy(at(1), at(0), base + 4, yp),
            2: copy(at(1), at(2), base + 5, ym),
            6: copy(at(7), at(6), base + 6, yp),
            8: copy(at(7), at(8), base + 7, ym),
        }

    cf = halo(hf, 32, 0)
    cb = halo(hb, 16, 8)
    cd = halo(hd, 32, 16)
    c_yp = copy(cp.at[2], ry.at[0], 24, yp)
    c_ym = copy(cp.at[0], ry.at[1], 25, ym)
    c_xp = copy(red.at[2], rx.at[0], 26, xp)
    c_xm = copy(red.at[0], rx.at[1], 27, xm)

    pl.semaphore_wait(barrier, 4)
    for k in (1, 7, 3, 5):
        cf[k].start()
    for k in (1, 7, 3, 5):
        cb[k].start()

    u_planes = [fvel[d] for d in range(3)]
    mf_live = jnp.where(f_on, fmass[...], 0.0)
    one1 = jnp.ones((1, 128), F32)
    zero3 = jnp.zeros((3, 128), F32)
    for b in range(32):
        s = slice(b, b + 1)
        v = jnp.concatenate(
            [one1, zero3, u_planes[0][s], u_planes[1][s], u_planes[2][s], zero3[:1]], axis=0
        )
        fu[b] = v
        fi[b] = v * row8(mf_live[s])

    zeros80 = jnp.zeros((80, 128), F32)

    def own_left(i, _):
        raw = hf[128 + i]
        x = raw - 0.5
        x1, x2, x3 = x[1:2], x[2:3], x[3:4]
        norm = -(x1 * x1 + x2 * x2 + x3 * x3)
        u8 = jnp.concatenate([norm, x1, x2, x3, one1, zero3], axis=0)
        full = jnp.concatenate([left_stack(u8), zeros80], axis=0)
        ut[i] = full.T.astype(BF16)
        return 0

    lax.fori_loop(0, 32, own_left, 0)


    for k in (1, 7):
        cf[k].wait_recv()
    for k in (0, 2, 6, 8):
        cf[k].start()
    for k in (1, 7):
        cb[k].wait_recv()
    for k in (0, 2, 6, 8):
        cb[k].start()
    for k in (3, 5, 0, 2, 6, 8):
        cf[k].wait_recv()

    coord = (row >= 1) & (row <= 3)
    fac = jnp.where(row == 0, INV_H2, 2.0 * INV_H2)
    ones8 = jnp.ones((8, 128), BF16)
    zeros4 = jnp.zeros((4, 128), F32)

    def density(i, _):
        lhs = ut[i][:, 0:48]
        acc = jnp.zeros((128, 128), F32)
        for jj in range(4):
            cols = []
            for h in range(2):
                j = jj * 2 + h
                nid = fl[i * 8 + j]
                ox, oy = tile_offsets(nid >> 5)
                raw = jnp.concatenate([hf[nid], zeros4], axis=0)
                shift = jnp.where(
                    row == 1, ox - 0.5, jnp.where(row == 2, oy - 0.5, -0.5)
                )
                x = jnp.where(coord, raw + shift, 0.0)
                c8 = row8(raw[0:1])
                n8 = jnp.sum(x * x, axis=0, keepdims=True)
                y = jnp.where(row == 0, c8, c8 * x)
                fx[i * 8 + j] = y
                w = jnp.where(row < 4, y * fac, jnp.where(row == 4, c8 * (1.0 - INV_H2 * n8), 0.0))
                cols.append(right_stack(w))
            u = jnp.maximum(dot(lhs, jnp.concatenate(cols, axis=1), NN), 0.0)
            sq = u * u
            cube = sq * u
            acc = acc + (cube[:, 0:128] + cube[:, 128:256])
            hi, lo = halves(sq)
            qh[i, :, jj * 256 : (jj + 1) * 256] = hi
            ql[i, :, jj * 256 : (jj + 1) * 256] = lo
        a, b, c = split3(acc)
        total = (
            dot(ones8, a.astype(BF16), NT)
            + dot(ones8, b.astype(BF16), NT)
            + dot(ones8, c.astype(BF16), NT)
        )
        dens[pl.ds(i, 1), :] = total[0:1]
        return 0

    lax.fori_loop(0, 32, density, 0)
    rho = fmass[...] + dens[...]
    weight = STIFF * (rho / REST - 1.0) / (rho * rho)
    for b in range(32):
        hd[128 + b] = weight[b : b + 1]
    for k in (1, 7, 3, 5):
        cd[k].start()
    o_fd[...] = jnp.where(f_on, rho, 0.0)

    for k in (3, 5, 0, 2, 6, 8):
        cb[k].wait_recv()
    fac2 = jnp.where(row == 0, 1.0, 2.0)

    def coupling(i, _):
        lhs = ut[i][:, 0:48]
        cols = []
        funs = []
        for j in range(4):
            nid = cl[i * 4 + j]
            ox, oy = tile_offsets(nid >> 4)
            raw = hb[nid]
            shift = jnp.where(row == 1, ox - 0.5, jnp.where(row == 2, oy - 0.5, -0.5))
            x = jnp.where(coord, raw + shift, 0.0)
            m8 = row8(raw[0:1])
            c8 = jnp.where(m8 > 0.0, jnp.sqrt(jnp.maximum(m8, 1e-30)), 0.0)
            reach = row8(raw[7:8]) + COUPLE
            t8 = 1.0 / (reach * reach)
            n8 = jnp.sum(x * x, axis=0, keepdims=True)
            y = jnp.where(row == 0, c8, c8 * x)
            w = jnp.where(row < 4, y * (t8 * fac2), jnp.where(row == 4, c8 * (1.0 - t8 * n8), 0.0))
            cols.append(right_stack(w))
            funs.append(stack3(jnp.where(row == 0, 1.0, raw)))
        fside = stack3(fi[i])
        pulled = jnp.zeros((24, 128), F32)
        for h in range(2):
            rhs = jnp.concatenate(cols[2 * h : 2 * h + 2], axis=1)
            u = jnp.maximum(dot(lhs, rhs, NN), 0.0)
            hi, lo = halves(u * u)
            fun = jnp.concatenate(funs[2 * h : 2 * h + 2], axis=1)
            pulled = pulled + dot(fun, hi, NT) + dot(fun, lo, NT)
            back = sum3(dot(fside, hi, NN) + dot(fside, lo, NN))
            for g in range(2):
                at = pl.ds(pl.multiple_of((i * 4 + 2 * h + g) * 8, 8), 8)
                sp[at, :] = back[:, g * 128 : (g + 1) * 128]
        d8 = sum3(pulled)
        drag = d8 - fu[i] * row8(d8[0:1])
        for d in range(3):
            dr[d, pl.ds(i, 1), :] = drag[4 + d : 5 + d]
        return 0

    lax.fori_loop(0, 32, coupling, 0)

    for k in (1, 7):
        cd[k].wait_recv()
    for k in (0, 2, 6, 8):
        cd[k].start()

    onehot = (
        lax.broadcasted_iota(jnp.int32, (144, 128), 0) == jnp.broadcast_to(clv[...], (144, 128))
    ).astype(F32).astype(BF16)

    def reduced(r):
        parts = split3(sp[pl.ds(r, 128, stride=8), :])
        m = jnp.concatenate([v.astype(BF16) for v in parts], axis=1)
        got = dot(onehot, m, NN)
        return got[:, 0:128] + got[:, 128:256] + got[:, 256:384]

    mass_sum = reduced(0)
    for d in range(3):
        vel = hb[:, 4 + d, :]
        part = reduced(4 + d) - vel * mass_sum
        for t in range(9):
            cp[t % 3, t // 3, d] = part[t * 16 : (t + 1) * 16]
    c_yp.start()
    c_ym.start()

    c_yp.wait_recv()
    c_ym.wait_recv()
    for g in range(3):
        red[g] = cp[1, g] + (ry[0, g] + ry[1, g])
    c_xp.start()
    c_xm.start()

    for k in (3, 5, 0, 2, 6, 8):
        cd[k].wait_recv()

    def pressure(i, _):
        got = jnp.zeros((24, 128), F32)
        for j in range(8):
            nid = fl[i * 8 + j]
            y = fx[i * 8 + j]
            w8 = row8(hd[nid])
            fun = stack3(jnp.concatenate([y[0:4], (y * w8)[0:4]], axis=0))
            at = slice(j * 128, (j + 1) * 128)
            got = got + dot(fun, qh[i, :, at], NT) + dot(fun, ql[i, :, at], NT)
        p8 = sum3(got)
        w_i = row8(hd[128 + i])
        comb = w_i[0:4] * p8[0:4] + p8[4:8]
        x = hf[128 + i] - 0.5
        force = x * jnp.broadcast_to(comb[0:1], (4, 128)) - comb
        for d in range(3):
            pf[d, pl.ds(i, 1), :] = force[d + 1 : d + 2]
        return 0

    lax.fori_loop(0, 32, pressure, 0)
    for d in range(3):
        down = -1.0 if d == 2 else 0.0
        o_fa[d] = jnp.where(f_on, PRESS_C * pf[d] + dr[d] + down, 0.0)

    c_xp.wait_recv()
    c_xm.wait_recv()
    for d in range(3):
        o_cp[d] = red[1, d] + (rx[0, d] + rx[1, d])

    for group in (cf, cb, cd):
        for k in group:
            group[k].wait_send()
    for c in (c_yp, c_ym, c_xp, c_xm):
        c.wait_send()


def contact_kernel(
    bcnt, bpos, bvel, brad, bmass, cid, hist, hb, coupled, o_ba, o_h, ga, cnb, pu
):
    for b in range(16):
        cnb[b : b + 1, :] = jnp.full((1, 128), bcnt[b], jnp.int32)

    def block(b, _):
        st = pl.multiple_of(b * 128, 128)
        ids8 = cid[:, pl.ds(st, 128)]
        for q in range(8):
            ids = row8(ids8[q : q + 1])
            ln = ids & 127
            bits = [(ids & (128 << k)) != 0 for k in range(4)]
            tl = ids >> 11
            out = None
            for t in range(9):
                vals = [
                    jnp.take_along_axis(
                        hb[t * 16 + r], ln, axis=1,
                        mode="promise_in_bounds",
                    )
                    for r in range(16)
                ]
                for k in range(4):
                    vals = [
                        jnp.where(bits[k], vals[j + 1], vals[j]) for j in range(0, len(vals), 2)
                    ]
                out = vals[0] if out is None else jnp.where(tl == t, vals[0], out)
            ga[q * 8 : q * 8 + 8, :] = out

        ox, oy = tile_offsets(ids8 >> 11)
        got = [ga[pl.ds(f, 8, stride=8), :] for f in range(8)]
        at = pl.ds(b, 1)
        r1 = row8(bpos[0, at, :]) - (got[1] + ox)
        r2 = row8(bpos[1, at, :]) - (got[2] + oy)
        r3 = row8(bpos[2, at, :]) - got[3]
        dist = jnp.sqrt((r1 * r1 + r2 * r2) + r3 * r3 + SOFT2)
        inv = 1.0 / dist
        nrm = (r1 * inv, r2 * inv, r3 * inv)
        inter = jnp.where(got[0] > 0.0, jnp.maximum(row8(brad[at, :]) + got[7] - dist, 0.0), 0.0)
        rel = [row8(bvel[d, at, :]) - got[4 + d] for d in range(3)]
        along = (rel[0] * nrm[0] + rel[1] * nrm[1]) + rel[2] * nrm[2]
        touch = jnp.minimum(inter * 100.0, 1.0)
        on = lax.broadcasted_iota(jnp.int32, (8, 128), 1) < jnp.broadcast_to(cnb[at, :], (8, 128))
        for d in range(3):
            spring = (hist[d, :, pl.ds(st, 128)] + DT * (rel[d] - along * nrm[d])) * touch
            push = NORMAL_K * inter * nrm[d] - SHEAR_K * spring
            pu[d, at, :] = jnp.sum(push, axis=0, keepdims=True)
            o_h[d, :, pl.ds(st, 128)] = jnp.where(on, spring, 0.0)
        return 0

    lax.fori_loop(0, 16, block, 0)
    b_on = lax.broadcasted_iota(jnp.int32, (16, 128), 1) < cnb[...]
    for d in range(3):
        down = -1.0 if d == 2 else 0.0
        o_ba[d] = jnp.where(b_on, (pu[d] + coupled[d]) / bmass[...] + down, 0.0)


def body(
    fluid_position, fluid_velocity, fluid_mass, fluid_counts, fluid_lists, coupling_lists,
    boulder_position, boulder_velocity, boulder_radius, boulder_mass, boulder_counts,
    contact_ids, spring_history,
):
    n_x, n_y = lax.axis_size("gx"), lax.axis_size("gy")
    vm = pl.BlockSpec(memory_space=pltpu.VMEM)
    sm = pl.BlockSpec(memory_space=pltpu.SMEM)
    counts_b = boulder_counts.reshape(16)
    pos_b = boulder_position.reshape(3, 16, 128)
    vel_b = boulder_velocity.reshape(3, 16, 128)
    rad_b = boulder_radius.reshape(16, 128)
    mass_b = boulder_mass.reshape(16, 128)
    fa, fd, hood, coupled = pl.pallas_call(
        lambda *refs: kernel(*refs, n_x=n_x, n_y=n_y),
        name="step",
        out_shape=(
            jax.ShapeDtypeStruct((3, 32, 128), F32),
            jax.ShapeDtypeStruct((32, 128), F32),
            jax.ShapeDtypeStruct((144, 8, 128), F32),
            jax.ShapeDtypeStruct((3, 16, 128), F32),
        ),
        in_specs=[sm] * 4 + [vm] * 8,
        out_specs=(vm,) * 4,
        scratch_shapes=[
            pltpu.VMEM((288, 4, 128), F32),
            pltpu.VMEM((288, 1, 128), F32),
            pltpu.VMEM((32, 128, 128), BF16),
            pltpu.VMEM((32, 128, 1024), BF16),
            pltpu.VMEM((32, 128, 1024), BF16),
            pltpu.VMEM((256, 8, 128), F32),
            pltpu.VMEM((32, 8, 128), F32),
            pltpu.VMEM((32, 8, 128), F32),
            pltpu.VMEM((1024, 128), F32),
            pltpu.VMEM((3, 3, 3, 16, 128), F32),
            pltpu.VMEM((2, 3, 3, 16, 128), F32),
            pltpu.VMEM((3, 3, 16, 128), F32),
            pltpu.VMEM((2, 3, 16, 128), F32),
            pltpu.VMEM((32, 128), jnp.int32),
            pltpu.VMEM((16, 128), jnp.int32),
            pltpu.VMEM((32, 128), F32),
            pltpu.VMEM((3, 32, 128), F32),
            pltpu.VMEM((3, 32, 128), F32),
            pltpu.SemaphoreType.DMA((28,)),
            pltpu.SemaphoreType.DMA((28,)),
        ],
        compiler_params=pltpu.CompilerParams(
            collective_id=0, has_side_effects=True, vmem_limit_bytes=48 * 1024 * 1024
        ),
    )(
        fluid_lists.reshape(256),
        coupling_lists.reshape(128),
        fluid_counts.reshape(32),
        counts_b,
        fluid_position.reshape(3, 32, 128),
        fluid_velocity.reshape(3, 32, 128),
        fluid_mass.reshape(32, 128),
        coupling_lists.reshape(1, 128),
        pos_b,
        vel_b,
        rad_b,
        mass_b,
    )
    ba, ho = pl.pallas_call(
        contact_kernel,
        name="contact",
        out_shape=(
            jax.ShapeDtypeStruct((3, 16, 128), F32),
            jax.ShapeDtypeStruct((3, 8, 2048), F32),
        ),
        in_specs=[sm] + [vm] * 8,
        out_specs=(vm,) * 2,
        scratch_shapes=[
            pltpu.VMEM((64, 128), F32),
            pltpu.VMEM((16, 128), jnp.int32),
            pltpu.VMEM((3, 16, 128), F32),
        ],
    )(
        counts_b, pos_b, vel_b, rad_b, mass_b,
        contact_ids.reshape(8, 2048), spring_history.reshape(3, 8, 2048), hood, coupled,
    )
    return (
        fa.reshape(3, 1, 1, 4096),
        fd.reshape(1, 1, 4096),
        ba.reshape(3, 1, 1, 2048),
        ho.reshape(3, 1, 1, 8, 2048),
    )


def solution(mesh):
    v4 = P(None, "gx", "gy", None)
    v3 = P("gx", "gy", None)
    l4 = P("gx", "gy", None, None)
    h5 = P(None, "gx", "gy", None, None)
    return jax.shard_map(
        body,
        mesh=mesh,
        in_specs=(v4, v4, v3, v3, l4, l4, v4, v4, v3, v3, v3, l4, h5),
        out_specs=(v4, v3, v4, h5),
        check_vma=False,
    )
```

```python
import jax
import jax.numpy as jnp
from jax import lax
from jax.experimental import pallas as pl
from jax.experimental.pallas import tpu as pltpu
from jax.sharding import PartitionSpec as P

F32 = jnp.float32
BF16 = jnp.bfloat16
MESH = pl.DeviceIdType.MESH
NT = (((1,), (1,)), ((), ()))
NN = (((1,), (0,)), ((), ()))

INV_H2 = 1.0 / 0.3**2
REST = 10.0
STIFF = 10.0
COUPLE = 0.1
NORMAL_K = 10.0
SHEAR_K = 20.0
DT = 0.05
SOFT2 = 0.02**2
PRESS_C = 6.0 / 0.3**2


def rounded(x):
    return x.astype(BF16).astype(F32)


def split3(x):
    hi = rounded(x)
    rest = x - hi
    mid = rounded(rest)
    return hi, mid, rest - mid


def dot(a, b, dims):
    return lax.dot_general(a, b, dims, preferred_element_type=F32)


def left_stack(x):
    h, m, l = split3(x)
    return jnp.concatenate([h, h, m, m, h, l], axis=0)


def right_stack(x):
    h, m, l = split3(x)
    return jnp.concatenate([h, m, h, m, l, h], axis=0).astype(BF16)


def stack3(x):
    return jnp.concatenate(split3(x), axis=0).astype(BF16)


def sum3(x):
    return x[0:8] + x[8:16] + x[16:24]


def row8(x):
    return jnp.broadcast_to(x, (8, x.shape[-1]))


def halves(x):
    hi = x.astype(BF16)
    return hi, (x - hi.astype(F32)).astype(BF16)


def tile_offsets(tile):
    third = (tile * 11) >> 5
    return (third - 1).astype(F32), (tile - 3 * third - 1).astype(F32)


def kernel(
    fl, cl, fcnt, bcnt,
    fpos, fvel, fmass, clv, bpos, bvel, brad, bmass, cid, hist,
    o_fa, o_fd, o_ba, o_h,
    hf, hb, hd, ut, qh, ql, fx, fu, fi, ga, sp, cp, ry, red, rx,
    cnf, cnb, dens, dr, pf, pu, ssem, rsem,
    *, n_x, n_y,
):
    me_x = lax.axis_index("gx")
    me_y = lax.axis_index("gy")
    xp = (lax.rem(me_x + 1, n_x), me_y)
    xm = (lax.rem(me_x + n_x - 1, n_x), me_y)
    yp = (me_x, lax.rem(me_y + 1, n_y))
    ym = (me_x, lax.rem(me_y + n_y - 1, n_y))

    barrier = pltpu.get_barrier_semaphore()
    for dev in (xp, xm, yp, ym):
        pl.semaphore_signal(barrier, inc=1, device_id=dev, device_id_type=MESH)

    row = lax.broadcasted_iota(jnp.int32, (8, 128), 0)
    lane = lax.broadcasted_iota(jnp.int32, (32, 128), 1)

    for b in range(32):
        cnf[b : b + 1, :] = jnp.full((1, 128), fcnt[b], jnp.int32)
    for b in range(16):
        cnb[b : b + 1, :] = jnp.full((1, 128), bcnt[b], jnp.int32)
    f_on = lane < cnf[...]
    b_on = lane[:16] < cnb[...]
    croot = jnp.where(f_on, jnp.exp(jnp.log(fmass[...]) * (1.0 / 3.0)), 0.0)
    for b in range(32):
        s = slice(b, b + 1)
        hf[128 + b] = jnp.concatenate(
            [croot[s], fpos[0, s, :], fpos[1, s, :], fpos[2, s, :]], axis=0
        )
    bm_live = jnp.where(b_on, bmass[...], 0.0)
    for b in range(16):
        s = slice(b, b + 1)
        hb[64 + b] = jnp.concatenate(
            [bm_live[s]]
            + [bpos[d, s, :] for d in range(3)]
            + [bvel[d, s, :] for d in range(3)]
            + [brad[s, :]],
            axis=0,
        )

    def copy(src, dst, k, dev):
        return pltpu.make_async_remote_copy(
            src_ref=src, dst_ref=dst, send_sem=ssem.at[k], recv_sem=rsem.at[k],
            device_id=dev, device_id_type=MESH,
        )

    def halo(ref, width, base):
        at = lambda t: ref.at[pl.ds(t * width, width)]
        return {
            1: copy(at(4), at(1), base + 0, xp),
            7: copy(at(4), at(7), base + 1, xm),
            3: copy(at(4), at(3), base + 2, yp),
            5: copy(at(4), at(5), base + 3, ym),
            0: copy(at(1), at(0), base + 4, yp),
            2: copy(at(1), at(2), base + 5, ym),
            6: copy(at(7), at(6), base + 6, yp),
            8: copy(at(7), at(8), base + 7, ym),
        }

    cf = halo(hf, 32, 0)
    cb = halo(hb, 16, 8)
    cd = halo(hd, 32, 16)
    c_yp = copy(cp.at[2], ry.at[0], 24, yp)
    c_ym = copy(cp.at[0], ry.at[1], 25, ym)
    c_xp = copy(red.at[2], rx.at[0], 26, xp)
    c_xm = copy(red.at[0], rx.at[1], 27, xm)

    pl.semaphore_wait(barrier, 4)
    for k in (1, 7, 3, 5):
        cf[k].start()
    for k in (1, 7, 3, 5):
        cb[k].start()

    u_planes = [fvel[d] for d in range(3)]
    mf_live = jnp.where(f_on, fmass[...], 0.0)
    one1 = jnp.ones((1, 128), F32)
    zero3 = jnp.zeros((3, 128), F32)
    for b in range(32):
        s = slice(b, b + 1)
        v = jnp.concatenate(
            [one1, zero3, u_planes[0][s], u_planes[1][s], u_planes[2][s], zero3[:1]], axis=0
        )
        fu[b] = v
        fi[b] = v * row8(mf_live[s])

    zeros80 = jnp.zeros((80, 128), F32)

    def own_left(i, _):
        raw = hf[128 + i]
        x = raw - 0.5
        x1, x2, x3 = x[1:2], x[2:3], x[3:4]
        norm = -(x1 * x1 + x2 * x2 + x3 * x3)
        u8 = jnp.concatenate([norm, x1, x2, x3, one1, zero3], axis=0)
        full = jnp.concatenate([left_stack(u8), zeros80], axis=0)
        ut[i] = full.T.astype(BF16)
        return 0

    lax.fori_loop(0, 32, own_left, 0)

    def gather(tiles, first):
        def block(b, _):
            st = pl.multiple_of(b * 128, 128)
            ids8 = cid[:, pl.ds(st, 128)]
            for q in range(8):
                ids = row8(ids8[q : q + 1])
                ln = ids & 127
                bits = [(ids & (128 << k)) != 0 for k in range(4)]
                tl = ids >> 11
                at = pl.ds(pl.multiple_of(b * 64 + q * 8, 8), 8)
                out = jnp.zeros((8, 128), F32) if first else ga[at, :]
                for t in tiles:
                    vals = [
                        jnp.take_along_axis(
                            hb[t * 16 + r], ln, axis=1,
                            mode="promise_in_bounds",
                        )
                        for r in range(16)
                    ]
                    for k in range(4):
                        vals = [
                            jnp.where(bits[k], vals[j + 1], vals[j]) for j in range(0, len(vals), 2)
                        ]
                    out = jnp.where(tl == t, vals[0], out)
                ga[at, :] = out
            return 0

        lax.fori_loop(0, 16, block, 0)

    gather((4,), True)
    cb[3].wait_recv()
    cb[5].wait_recv()
    gather((3, 5), False)

    for k in (1, 7):
        cf[k].wait_recv()
    for k in (0, 2, 6, 8):
        cf[k].start()
    for k in (1, 7):
        cb[k].wait_recv()
    for k in (0, 2, 6, 8):
        cb[k].start()
    for k in (3, 5, 0, 2, 6, 8):
        cf[k].wait_recv()

    coord = (row >= 1) & (row <= 3)
    fac = jnp.where(row == 0, INV_H2, 2.0 * INV_H2)
    ones8 = jnp.ones((8, 128), BF16)
    zeros4 = jnp.zeros((4, 128), F32)

    def density(i, _):
        lhs = ut[i][:, 0:48]
        acc = jnp.zeros((128, 128), F32)
        for jj in range(4):
            cols = []
            for h in range(2):
                j = jj * 2 + h
                nid = fl[i * 8 + j]
                ox, oy = tile_offsets(nid >> 5)
                raw = jnp.concatenate([hf[nid], zeros4], axis=0)
                shift = jnp.where(
                    row == 1, ox - 0.5, jnp.where(row == 2, oy - 0.5, -0.5)
                )
                x = jnp.where(coord, raw + shift, 0.0)
                c8 = row8(raw[0:1])
                n8 = jnp.sum(x * x, axis=0, keepdims=True)
                y = jnp.where(row == 0, c8, c8 * x)
                fx[i * 8 + j] = y
                w = jnp.where(row < 4, y * fac, jnp.where(row == 4, c8 * (1.0 - INV_H2 * n8), 0.0))
                cols.append(right_stack(w))
            u = jnp.maximum(dot(lhs, jnp.concatenate(cols, axis=1), NN), 0.0)
            sq = u * u
            cube = sq * u
            acc = acc + (cube[:, 0:128] + cube[:, 128:256])
            hi, lo = halves(sq)
            qh[i, :, jj * 256 : (jj + 1) * 256] = hi
            ql[i, :, jj * 256 : (jj + 1) * 256] = lo
        a, b, c = split3(acc)
        total = (
            dot(ones8, a.astype(BF16), NT)
            + dot(ones8, b.astype(BF16), NT)
            + dot(ones8, c.astype(BF16), NT)
        )
        dens[pl.ds(i, 1), :] = total[0:1]
        return 0

    lax.fori_loop(0, 32, density, 0)
    rho = fmass[...] + dens[...]
    weight = STIFF * (rho / REST - 1.0) / (rho * rho)
    for b in range(32):
        hd[128 + b] = weight[b : b + 1]
    for k in (1, 7, 3, 5):
        cd[k].start()
    o_fd[...] = jnp.where(f_on, rho, 0.0)

    for k in (0, 2, 6, 8):
        cb[k].wait_recv()
    fac2 = jnp.where(row == 0, 1.0, 2.0)

    def coupling(i, _):
        lhs = ut[i][:, 0:48]
        cols = []
        funs = []
        for j in range(4):
            nid = cl[i * 4 + j]
            ox, oy = tile_offsets(nid >> 4)
            raw = hb[nid]
            shift = jnp.where(row == 1, ox - 0.5, jnp.where(row == 2, oy - 0.5, -0.5))
            x = jnp.where(coord, raw + shift, 0.0)
            m8 = row8(raw[0:1])
            c8 = jnp.where(m8 > 0.0, jnp.sqrt(jnp.maximum(m8, 1e-30)), 0.0)
            reach = row8(raw[7:8]) + COUPLE
            t8 = 1.0 / (reach * reach)
            n8 = jnp.sum(x * x, axis=0, keepdims=True)
            y = jnp.where(row == 0, c8, c8 * x)
            w = jnp.where(row < 4, y * (t8 * fac2), jnp.where(row == 4, c8 * (1.0 - t8 * n8), 0.0))
            cols.append(right_stack(w))
            funs.append(stack3(jnp.where(row == 0, 1.0, raw)))
        fside = stack3(fi[i])
        pulled = jnp.zeros((24, 128), F32)
        for h in range(2):
            rhs = jnp.concatenate(cols[2 * h : 2 * h + 2], axis=1)
            u = jnp.maximum(dot(lhs, rhs, NN), 0.0)
            hi, lo = halves(u * u)
            fun = jnp.concatenate(funs[2 * h : 2 * h + 2], axis=1)
            pulled = pulled + dot(fun, hi, NT) + dot(fun, lo, NT)
            back = sum3(dot(fside, hi, NN) + dot(fside, lo, NN))
            for g in range(2):
                at = pl.ds(pl.multiple_of((i * 4 + 2 * h + g) * 8, 8), 8)
                sp[at, :] = back[:, g * 128 : (g + 1) * 128]
        d8 = sum3(pulled)
        drag = d8 - fu[i] * row8(d8[0:1])
        for d in range(3):
            dr[d, pl.ds(i, 1), :] = drag[4 + d : 5 + d]
        return 0

    lax.fori_loop(0, 32, coupling, 0)

    for k in (1, 7):
        cd[k].wait_recv()
    for k in (0, 2, 6, 8):
        cd[k].start()

    onehot = (
        lax.broadcasted_iota(jnp.int32, (144, 128), 0) == jnp.broadcast_to(clv[...], (144, 128))
    ).astype(F32).astype(BF16)

    def reduced(r):
        parts = split3(sp[pl.ds(r, 128, stride=8), :])
        m = jnp.concatenate([v.astype(BF16) for v in parts], axis=1)
        got = dot(onehot, m, NN)
        return got[:, 0:128] + got[:, 128:256] + got[:, 256:384]

    mass_sum = reduced(0)
    for d in range(3):
        vel = hb[:, 4 + d, :]
        part = reduced(4 + d) - vel * mass_sum
        for t in range(9):
            cp[t % 3, t // 3, d] = part[t * 16 : (t + 1) * 16]
    c_yp.start()
    c_ym.start()

    gather((1, 7), False)

    c_yp.wait_recv()
    c_ym.wait_recv()
    for g in range(3):
        red[g] = cp[1, g] + (ry[0, g] + ry[1, g])
    c_xp.start()
    c_xm.start()

    gather((0, 2, 6, 8), False)

    def contact(b, _):
        st = pl.multiple_of(b * 128, 128)
        ids = cid[:, pl.ds(st, 128)]
        ox, oy = tile_offsets(ids >> 11)
        base = b * 64
        got = [ga[pl.ds(base + f, 8, stride=8), :] for f in range(8)]
        at = pl.ds(b, 1)
        r1 = row8(bpos[0, at, :]) - (got[1] + ox)
        r2 = row8(bpos[1, at, :]) - (got[2] + oy)
        r3 = row8(bpos[2, at, :]) - got[3]
        dist = jnp.sqrt((r1 * r1 + r2 * r2) + r3 * r3 + SOFT2)
        inv = 1.0 / dist
        nrm = (r1 * inv, r2 * inv, r3 * inv)
        inter = jnp.where(got[0] > 0.0, jnp.maximum(row8(brad[at, :]) + got[7] - dist, 0.0), 0.0)
        rel = [row8(bvel[d, at, :]) - got[4 + d] for d in range(3)]
        along = (rel[0] * nrm[0] + rel[1] * nrm[1]) + rel[2] * nrm[2]
        touch = jnp.minimum(inter * 100.0, 1.0)
        on = lax.broadcasted_iota(jnp.int32, (8, 128), 1) < jnp.broadcast_to(cnb[at, :], (8, 128))
        for d in range(3):
            spring = (hist[d, :, pl.ds(st, 128)] + DT * (rel[d] - along * nrm[d])) * touch
            push = NORMAL_K * inter * nrm[d] - SHEAR_K * spring
            pu[d, at, :] = jnp.sum(push, axis=0, keepdims=True)
            o_h[d, :, pl.ds(st, 128)] = jnp.where(on, spring, 0.0)
        return 0

    lax.fori_loop(0, 16, contact, 0)

    for k in (3, 5, 0, 2, 6, 8):
        cd[k].wait_recv()

    def pressure(i, _):
        got = jnp.zeros((24, 128), F32)
        for j in range(8):
            nid = fl[i * 8 + j]
            y = fx[i * 8 + j]
            w8 = row8(hd[nid])
            fun = stack3(jnp.concatenate([y[0:4], (y * w8)[0:4]], axis=0))
            at = slice(j * 128, (j + 1) * 128)
            got = got + dot(fun, qh[i, :, at], NT) + dot(fun, ql[i, :, at], NT)
        p8 = sum3(got)
        w_i = row8(hd[128 + i])
        comb = w_i[0:4] * p8[0:4] + p8[4:8]
        x = hf[128 + i] - 0.5
        force = x * jnp.broadcast_to(comb[0:1], (4, 128)) - comb
        for d in range(3):
            pf[d, pl.ds(i, 1), :] = force[d + 1 : d + 2]
        return 0

    lax.fori_loop(0, 32, pressure, 0)
    for d in range(3):
        down = -1.0 if d == 2 else 0.0
        o_fa[d] = jnp.where(f_on, PRESS_C * pf[d] + dr[d] + down, 0.0)

    c_xp.wait_recv()
    c_xm.wait_recv()
    for d in range(3):
        down = -1.0 if d == 2 else 0.0
        coupled = red[1, d] + (rx[0, d] + rx[1, d])
        o_ba[d] = jnp.where(b_on, (pu[d] + coupled) / bmass[...] + down, 0.0)

    for group in (cf, cb, cd):
        for k in group:
            group[k].wait_send()
    for c in (c_yp, c_ym, c_xp, c_xm):
        c.wait_send()


def body(
    fluid_position, fluid_velocity, fluid_mass, fluid_counts, fluid_lists, coupling_lists,
    boulder_position, boulder_velocity, boulder_radius, boulder_mass, boulder_counts,
    contact_ids, spring_history,
):
    n_x, n_y = lax.axis_size("gx"), lax.axis_size("gy")
    vm = pl.BlockSpec(memory_space=pltpu.VMEM)
    sm = pl.BlockSpec(memory_space=pltpu.SMEM)
    outs = pl.pallas_call(
        lambda *refs: kernel(*refs, n_x=n_x, n_y=n_y),
        name="step",
        out_shape=(
            jax.ShapeDtypeStruct((3, 32, 128), F32),
            jax.ShapeDtypeStruct((32, 128), F32),
            jax.ShapeDtypeStruct((3, 16, 128), F32),
            jax.ShapeDtypeStruct((3, 8, 2048), F32),
        ),
        in_specs=[sm] * 4 + [vm] * 10,
        out_specs=(vm,) * 4,
        scratch_shapes=[
            pltpu.VMEM((288, 4, 128), F32),
            pltpu.VMEM((144, 8, 128), F32),
            pltpu.VMEM((288, 1, 128), F32),
            pltpu.VMEM((32, 128, 128), BF16),
            pltpu.VMEM((32, 128, 1024), BF16),
            pltpu.VMEM((32, 128, 1024), BF16),
            pltpu.VMEM((256, 8, 128), F32),
            pltpu.VMEM((32, 8, 128), F32),
            pltpu.VMEM((32, 8, 128), F32),
            pltpu.VMEM((1024, 128), F32),
            pltpu.VMEM((1024, 128), F32),
            pltpu.VMEM((3, 3, 3, 16, 128), F32),
            pltpu.VMEM((2, 3, 3, 16, 128), F32),
            pltpu.VMEM((3, 3, 16, 128), F32),
            pltpu.VMEM((2, 3, 16, 128), F32),
            pltpu.VMEM((32, 128), jnp.int32),
            pltpu.VMEM((16, 128), jnp.int32),
            pltpu.VMEM((32, 128), F32),
            pltpu.VMEM((3, 32, 128), F32),
            pltpu.VMEM((3, 32, 128), F32),
            pltpu.VMEM((3, 16, 128), F32),
            pltpu.SemaphoreType.DMA((28,)),
            pltpu.SemaphoreType.DMA((28,)),
        ],
        compiler_params=pltpu.CompilerParams(
            collective_id=0, has_side_effects=True, vmem_limit_bytes=67043328
        ),
    )(
        fluid_lists.reshape(256),
        coupling_lists.reshape(128),
        fluid_counts.reshape(32),
        boulder_counts.reshape(16),
        fluid_position.reshape(3, 32, 128),
        fluid_velocity.reshape(3, 32, 128),
        fluid_mass.reshape(32, 128),
        coupling_lists.reshape(1, 128),
        boulder_position.reshape(3, 16, 128),
        boulder_velocity.reshape(3, 16, 128),
        boulder_radius.reshape(16, 128),
        boulder_mass.reshape(16, 128),
        contact_ids.reshape(8, 2048),
        spring_history.reshape(3, 8, 2048),
    )
    fa, fd, ba, ho = outs
    return (
        fa.reshape(3, 1, 1, 4096),
        fd.reshape(1, 1, 4096),
        ba.reshape(3, 1, 1, 2048),
        ho.reshape(3, 1, 1, 8, 2048),
    )


def solution(mesh):
    v4 = P(None, "gx", "gy", None)
    v3 = P("gx", "gy", None)
    l4 = P("gx", "gy", None, None)
    h5 = P(None, "gx", "gy", None, None)
    return jax.shard_map(
        body,
        mesh=mesh,
        in_specs=(v4, v4, v3, v3, l4, l4, v4, v4, v3, v3, v3, l4, h5),
        out_specs=(v4, v3, v4, h5),
        check_vma=False,
    )
```

```python
import jax
import jax.numpy as jnp
from jax import lax
from jax.experimental import pallas as pl
from jax.experimental.pallas import tpu as pltpu
from jax.sharding import PartitionSpec as P

F32 = jnp.float32
BF16 = jnp.bfloat16
MESH = pl.DeviceIdType.MESH
NT = (((1,), (1,)), ((), ()))
NN = (((1,), (0,)), ((), ()))

INV_H2 = 1.0 / 0.3**2
REST = 10.0
STIFF = 10.0
COUPLE = 0.1
NORMAL_K = 10.0
SHEAR_K = 20.0
DT = 0.05
SOFT2 = 0.02**2
PRESS_C = 6.0 / 0.3**2
X_UNIT = 2.0**21
V_HALF = 32766
R_LOW = 0.03
R_UNIT = ((1 << 17) - 4) / 0.04


def rounded(x):
    return x.astype(BF16).astype(F32)


def split3(x):
    hi = rounded(x)
    rest = x - hi
    mid = rounded(rest)
    return hi, mid, rest - mid


def dot(a, b, dims):
    return lax.dot_general(a, b, dims, preferred_element_type=F32)


def left_stack(x):
    h, m, l = split3(x)
    return jnp.concatenate([h, h, m, m, h, l], axis=0)


def right_stack(x):
    h, m, l = split3(x)
    return jnp.concatenate([h, m, h, m, l, h], axis=0).astype(BF16)


def stack2(x):
    hi = rounded(x)
    return jnp.concatenate([hi, x - hi], axis=0).astype(BF16)


def sum2(x):
    return x[0:8] + x[8:16]


def row8(x):
    return jnp.broadcast_to(x, (8, x.shape[-1]))


def halves(x):
    hi = x.astype(BF16)
    return hi, (x - hi.astype(F32)).astype(BF16)


def tile_offsets(tile):
    third = (tile * 11) >> 5
    return (third - 1).astype(F32), (tile - 3 * third - 1).astype(F32)


def kernel(
    fl, cl, fcnt, bcnt,
    fpos, fvel, fmass, clv, bpos, bvel, brad, bmass, cid, hist,
    o_fa, o_fd, o_ba, o_h,
    hf, hb, hd, ut, qh, ql, fx, fu, fi, hp, sc, ga, sp, cp, ry, red, rx,
    cnf, cnb, dens, dr, pf, pu, ssem, rsem,
    *, n_x, n_y,
):
    me_x = lax.axis_index("gx")
    me_y = lax.axis_index("gy")
    xp = (lax.rem(me_x + 1, n_x), me_y)
    xm = (lax.rem(me_x + n_x - 1, n_x), me_y)
    yp = (me_x, lax.rem(me_y + 1, n_y))
    ym = (me_x, lax.rem(me_y + n_y - 1, n_y))

    barrier = pltpu.get_barrier_semaphore()
    for dev in (xp, xm, yp, ym):
        pl.semaphore_signal(barrier, inc=1, device_id=dev, device_id_type=MESH)

    row = lax.broadcasted_iota(jnp.int32, (8, 128), 0)
    lane = lax.broadcasted_iota(jnp.int32, (32, 128), 1)

    for b in range(32):
        cnf[b : b + 1, :] = jnp.full((1, 128), fcnt[b], jnp.int32)
    for b in range(16):
        cnb[b : b + 1, :] = jnp.full((1, 128), bcnt[b], jnp.int32)
    f_on = lane < cnf[...]
    b_on = lane[:16] < cnb[...]
    croot = jnp.where(f_on, jnp.exp(jnp.log(fmass[...]) * (1.0 / 3.0)), 0.0)
    for b in range(32):
        s = slice(b, b + 1)
        hf[128 + b] = jnp.concatenate(
            [croot[s], fpos[0, s, :], fpos[1, s, :], fpos[2, s, :]], axis=0
        )
    bm_live = jnp.where(b_on, bmass[...], 0.0)
    for b in range(16):
        s = slice(b, b + 1)
        hb[64 + b] = jnp.concatenate(
            [bm_live[s]]
            + [bpos[d, s, :] for d in range(3)]
            + [bvel[d, s, :] for d in range(3)]
            + [brad[s, :]],
            axis=0,
        )

    def copy(src, dst, k, dev):
        return pltpu.make_async_remote_copy(
            src_ref=src, dst_ref=dst, send_sem=ssem.at[k], recv_sem=rsem.at[k],
            device_id=dev, device_id_type=MESH,
        )

    def halo(ref, width, base):
        at = lambda t: ref.at[pl.ds(t * width, width)]
        return {
            1: copy(at(4), at(1), base + 0, xp),
            7: copy(at(4), at(7), base + 1, xm),
            3: copy(at(4), at(3), base + 2, yp),
            5: copy(at(4), at(5), base + 3, ym),
            0: copy(at(1), at(0), base + 4, yp),
            2: copy(at(1), at(2), base + 5, ym),
            6: copy(at(7), at(6), base + 6, yp),
            8: copy(at(7), at(8), base + 7, ym),
        }

    cf = halo(hf, 32, 0)
    cb = halo(hb, 16, 8)
    cd = halo(hd, 32, 16)
    c_yp = copy(cp.at[2], ry.at[0], 24, yp)
    c_ym = copy(cp.at[0], ry.at[1], 25, ym)
    c_xp = copy(red.at[2], rx.at[0], 26, xp)
    c_xm = copy(red.at[0], rx.at[1], 27, xm)

    u_planes = [fvel[d] for d in range(3)]
    mf_live = jnp.where(f_on, fmass[...], 0.0)
    one1 = jnp.ones((1, 128), F32)
    zero3 = jnp.zeros((3, 128), F32)
    for b in range(32):
        s = slice(b, b + 1)
        v = jnp.concatenate(
            [one1, zero3, u_planes[0][s], u_planes[1][s], u_planes[2][s], zero3[:1]], axis=0
        )
        fu[b] = v
        fi[b] = v * row8(mf_live[s])

    zeros80 = jnp.zeros((80, 128), F32)

    def own_left(i, _):
        raw = hf[128 + i]
        x = raw - 0.5
        x1, x2, x3 = x[1:2], x[2:3], x[3:4]
        norm = -(x1 * x1 + x2 * x2 + x3 * x3)
        u8 = jnp.concatenate([norm, x1, x2, x3, one1, zero3], axis=0)
        full = jnp.concatenate([left_stack(u8), zeros80], axis=0)
        ut[i] = full.T.astype(BF16)
        return 0

    lax.fori_loop(0, 32, own_left, 0)

    pl.semaphore_wait(barrier, 4)
    for k in (1, 7, 3, 5):
        cf[k].start()
    for k in (1, 7, 3, 5):
        cb[k].start()

    def pack(t):
        at = slice(t * 16, (t + 1) * 16)
        plane = lambda f: hb[at, f, :]
        vel = [plane(4 + d) for d in range(3)]
        top = jnp.maximum(jnp.maximum(jnp.abs(vel[0]), jnp.abs(vel[1])), jnp.abs(vel[2]))
        top = jnp.max(jnp.max(top, axis=0, keepdims=True), axis=1, keepdims=True)
        top = jnp.maximum(jnp.broadcast_to(top, (8, 128)), 1e-30)
        sc[t] = top * (1.0 / V_HALF)
        inv = V_HALF / top[0:1]
        coord = [
            jnp.minimum((plane(1 + d) * X_UNIT).astype(jnp.int32), (1 << 21) - 1) for d in range(3)
        ]
        code = [(v * inv + (V_HALF + 1.5)).astype(jnp.int32) for v in vel]
        rad = (jnp.maximum(plane(7) - R_LOW, 0.0) * R_UNIT + 1.5).astype(jnp.int32)
        rad = jnp.where(plane(0) > 0.0, jnp.minimum(rad, (1 << 17) - 1), 0)
        words = [(coord[d] << 11) | (code[d] >> 5) for d in range(3)]
        words.append(
            (rad << 15) | ((code[0] & 31) << 10) | ((code[1] & 31) << 5) | (code[2] & 31)
        )
        for w in range(4):
            for half in range(2):
                hp[pl.ds(t * 128 + half * 4 + w, 16, stride=8), :] = words[w]

    def gather(tiles, first):
        for t in tiles:
            pack(t)

        def block(b, _):
            st = pl.multiple_of(b * 128, 128)
            ids8 = cid[:, pl.ds(st, 128)]
            for q in range(4):
                ids = jnp.where(row < 4, row8(ids8[2 * q : 2 * q + 1]), row8(ids8[2 * q + 1 : 2 * q + 2]))
                ln = ids & 127
                bits = [(ids & (128 << k)) != 0 for k in range(4)]
                tl = ids >> 11
                at = pl.ds(pl.multiple_of(b * 32 + q * 8, 8), 8)
                out = None if first else ga[at, :]
                for t in tiles:
                    vals = [
                        jnp.take_along_axis(
                            hp[(t * 16 + r) * 8 : (t * 16 + r + 1) * 8, :], ln, axis=1,
                            mode="promise_in_bounds",
                        )
                        for r in range(16)
                    ]
                    for k in range(4):
                        vals = [
                            jnp.where(bits[k], vals[j + 1], vals[j]) for j in range(0, len(vals), 2)
                        ]
                    out = vals[0] if out is None else jnp.where(tl == t, vals[0], out)
                ga[at, :] = out
            return 0

        lax.fori_loop(0, 16, block, 0)

    gather((4,), True)
    cb[3].wait_recv()
    cb[5].wait_recv()
    gather((3, 5), False)

    for k in (1, 7):
        cf[k].wait_recv()
    for k in (0, 2, 6, 8):
        cf[k].start()
    for k in (3, 5, 0, 2, 6, 8):
        cf[k].wait_recv()

    coord = (row >= 1) & (row <= 3)
    fac = jnp.where(row == 0, INV_H2, 2.0 * INV_H2)
    ones8 = jnp.ones((8, 128), BF16)
    zeros4 = jnp.zeros((4, 128), F32)

    def density(i, _):
        lhs = ut[i][:, 0:48]
        acc = jnp.zeros((128, 128), F32)
        for jj in range(4):
            cols = []
            for h in range(2):
                j = jj * 2 + h
                nid = fl[i * 8 + j]
                ox, oy = tile_offsets(nid >> 5)
                raw = jnp.concatenate([hf[nid], zeros4], axis=0)
                shift = jnp.where(
                    row == 1, ox - 0.5, jnp.where(row == 2, oy - 0.5, -0.5)
                )
                x = jnp.where(coord, raw + shift, 0.0)
                c8 = row8(raw[0:1])
                n8 = jnp.sum(x * x, axis=0, keepdims=True)
                y = jnp.where(row == 0, c8, c8 * x)
                fx[i * 8 + j] = y
                w = jnp.where(row < 4, y * fac, jnp.where(row == 4, c8 * (1.0 - INV_H2 * n8), 0.0))
                cols.append(right_stack(w))
            u = jnp.maximum(dot(lhs, jnp.concatenate(cols, axis=1), NN), 0.0)
            sq = u * u
            cube = sq * u
            acc = acc + (cube[:, 0:128] + cube[:, 128:256])
            hi, lo = halves(sq)
            qh[i, :, jj * 256 : (jj + 1) * 256] = hi
            ql[i, :, jj * 256 : (jj + 1) * 256] = lo
        a, b, c = split3(acc)
        total = (
            dot(ones8, a.astype(BF16), NT)
            + dot(ones8, b.astype(BF16), NT)
            + dot(ones8, c.astype(BF16), NT)
        )
        dens[pl.ds(i, 1), :] = total[0:1]
        return 0

    lax.fori_loop(0, 16, density, 0)
    for k in (1, 7):
        cb[k].wait_recv()
    for k in (0, 2, 6, 8):
        cb[k].start()
    lax.fori_loop(16, 32, density, 0)
    rho = fmass[...] + dens[...]
    weight = STIFF * (rho / REST - 1.0) / (rho * rho)
    for b in range(32):
        hd[128 + b] = weight[b : b + 1]
    for k in (1, 7, 3, 5):
        cd[k].start()
    o_fd[...] = jnp.where(f_on, rho, 0.0)

    for k in (0, 2, 6, 8):
        cb[k].wait_recv()
    fac2 = jnp.where(row == 0, 1.0, 2.0)

    def coupling(i, _):
        lhs = ut[i][:, 0:48]
        cols = []
        funs = []
        for j in range(4):
            nid = cl[i * 4 + j]
            ox, oy = tile_offsets(nid >> 4)
            raw = hb[nid]
            shift = jnp.where(row == 1, ox - 0.5, jnp.where(row == 2, oy - 0.5, -0.5))
            x = jnp.where(coord, raw + shift, 0.0)
            m8 = row8(raw[0:1])
            c8 = jnp.where(m8 > 0.0, jnp.sqrt(jnp.maximum(m8, 1e-30)), 0.0)
            reach = row8(raw[7:8]) + COUPLE
            t8 = 1.0 / (reach * reach)
            n8 = jnp.sum(x * x, axis=0, keepdims=True)
            y = jnp.where(row == 0, c8, c8 * x)
            w = jnp.where(row < 4, y * (t8 * fac2), jnp.where(row == 4, c8 * (1.0 - t8 * n8), 0.0))
            cols.append(right_stack(w))
            funs.append(stack2(jnp.where(row == 0, 1.0, raw)))
        fside = stack2(fi[i])
        pulled = jnp.zeros((16, 128), F32)
        for h in range(2):
            rhs = jnp.concatenate(cols[2 * h : 2 * h + 2], axis=1)
            u = jnp.maximum(dot(lhs, rhs, NN), 0.0)
            hi, lo = halves(u * u)
            fun = jnp.concatenate(funs[2 * h : 2 * h + 2], axis=1)
            pulled = pulled + dot(fun, hi, NT) + dot(fun, lo, NT)
            back = sum2(dot(fside, hi, NN) + dot(fside, lo, NN))
            for g in range(2):
                at = pl.ds(pl.multiple_of((i * 4 + 2 * h + g) * 8, 8), 8)
                sp[at, :] = back[:, g * 128 : (g + 1) * 128]
        d8 = sum2(pulled)
        drag = d8 - fu[i] * row8(d8[0:1])
        for d in range(3):
            dr[d, pl.ds(i, 1), :] = drag[4 + d : 5 + d]
        return 0

    lax.fori_loop(0, 20, coupling, 0)
    for k in (1, 7):
        cd[k].wait_recv()
    for k in (0, 2, 6, 8):
        cd[k].start()
    lax.fori_loop(20, 32, coupling, 0)

    onehot = (
        lax.broadcasted_iota(jnp.int32, (144, 128), 0) == jnp.broadcast_to(clv[...], (144, 128))
    ).astype(F32).astype(BF16)

    def reduced(r):
        parts = split3(sp[pl.ds(r, 128, stride=8), :])
        m = jnp.concatenate([v.astype(BF16) for v in parts], axis=1)
        got = dot(onehot, m, NN)
        return got[:, 0:128] + got[:, 128:256] + got[:, 256:384]

    mass_sum = reduced(0)
    for d in range(3):
        vel = hb[:, 4 + d, :]
        part = reduced(4 + d) - vel * mass_sum
        for t in range(9):
            cp[t % 3, t // 3, d] = part[t * 16 : (t + 1) * 16]
    c_yp.start()
    c_ym.start()

    for k in (3, 5, 0, 2, 6, 8):
        cd[k].wait_recv()

    def pressure(i, _):
        got = jnp.zeros((16, 128), F32)
        for j in range(8):
            nid = fl[i * 8 + j]
            y = fx[i * 8 + j]
            w8 = row8(hd[nid])
            fun = stack2(jnp.concatenate([y[0:4], (y * w8)[0:4]], axis=0))
            at = slice(j * 128, (j + 1) * 128)
            got = got + dot(fun, qh[i, :, at], NT) + dot(fun, ql[i, :, at], NT)
        p8 = sum2(got)
        w_i = row8(hd[128 + i])
        comb = w_i[0:4] * p8[0:4] + p8[4:8]
        x = hf[128 + i] - 0.5
        force = x * jnp.broadcast_to(comb[0:1], (4, 128)) - comb
        for d in range(3):
            pf[d, pl.ds(i, 1), :] = force[d + 1 : d + 2]
        return 0

    lax.fori_loop(0, 14, pressure, 0)
    c_yp.wait_recv()
    c_ym.wait_recv()
    for g in range(3):
        red[g] = cp[1, g] + (ry[0, g] + ry[1, g])
    c_xp.start()
    c_xm.start()

    lax.fori_loop(14, 32, pressure, 0)
    for d in range(3):
        down = -1.0 if d == 2 else 0.0
        o_fa[d] = jnp.where(f_on, PRESS_C * pf[d] + dr[d] + down, 0.0)

    gather((1, 7), False)
    gather((0, 2, 6, 8), False)

    def contact(b, _):
        st = pl.multiple_of(b * 128, 128)
        ids = cid[:, pl.ds(st, 128)]
        tile = ids >> 11
        ox, oy = tile_offsets(tile)
        base = b * 32
        words = [ga[pl.ds(base + w, 8, stride=4), :] for w in range(4)]
        step = sc[0]
        for t in range(1, 9):
            step = jnp.where(tile == t, sc[t], step)
        low = words[3]
        xyz = [
            ((words[d] >> 11) & ((1 << 21) - 1)).astype(F32) * (1.0 / X_UNIT) + 0.5 / X_UNIT
            for d in range(3)
        ]
        pvel = [
            ((((words[d] & 2047) << 5) | ((low >> (10 - 5 * d)) & 31)) - (V_HALF + 1)).astype(F32)
            * step
            for d in range(3)
        ]
        code = (low >> 15) & ((1 << 17) - 1)
        prad = (code - 1).astype(F32) * (1.0 / R_UNIT) + R_LOW
        at = pl.ds(b, 1)
        r1 = row8(bpos[0, at, :]) - (xyz[0] + ox)
        r2 = row8(bpos[1, at, :]) - (xyz[1] + oy)
        r3 = row8(bpos[2, at, :]) - xyz[2]
        dist = jnp.sqrt((r1 * r1 + r2 * r2) + r3 * r3 + SOFT2)
        inv = 1.0 / dist
        nrm = (r1 * inv, r2 * inv, r3 * inv)
        inter = jnp.where(code > 0, jnp.maximum(row8(brad[at, :]) + prad - dist, 0.0), 0.0)
        rel = [row8(bvel[d, at, :]) - pvel[d] for d in range(3)]
        along = (rel[0] * nrm[0] + rel[1] * nrm[1]) + rel[2] * nrm[2]
        touch = jnp.minimum(inter * 100.0, 1.0)
        on = lax.broadcasted_iota(jnp.int32, (8, 128), 1) < jnp.broadcast_to(cnb[at, :], (8, 128))
        for d in range(3):
            spring = (hist[d, :, pl.ds(st, 128)] + DT * (rel[d] - along * nrm[d])) * touch
            push = NORMAL_K * inter * nrm[d] - SHEAR_K * spring
            pu[d, at, :] = jnp.sum(push, axis=0, keepdims=True)
            o_h[d, :, pl.ds(st, 128)] = jnp.where(on, spring, 0.0)
        return 0

    lax.fori_loop(0, 16, contact, 0)

    c_xp.wait_recv()
    c_xm.wait_recv()
    for d in range(3):
        down = -1.0 if d == 2 else 0.0
        coupled = red[1, d] + (rx[0, d] + rx[1, d])
        o_ba[d] = jnp.where(b_on, (pu[d] + coupled) / bmass[...] + down, 0.0)

    for group in (cf, cb, cd):
        for k in group:
            group[k].wait_send()
    for c in (c_yp, c_ym, c_xp, c_xm):
        c.wait_send()


def body(
    fluid_position, fluid_velocity, fluid_mass, fluid_counts, fluid_lists, coupling_lists,
    boulder_position, boulder_velocity, boulder_radius, boulder_mass, boulder_counts,
    contact_ids, spring_history,
):
    n_x, n_y = lax.axis_size("gx"), lax.axis_size("gy")
    vm = pl.BlockSpec(memory_space=pltpu.VMEM)
    sm = pl.BlockSpec(memory_space=pltpu.SMEM)
    outs = pl.pallas_call(
        lambda *refs: kernel(*refs, n_x=n_x, n_y=n_y),
        name="step",
        out_shape=(
            jax.ShapeDtypeStruct((3, 32, 128), F32),
            jax.ShapeDtypeStruct((32, 128), F32),
            jax.ShapeDtypeStruct((3, 16, 128), F32),
            jax.ShapeDtypeStruct((3, 8, 2048), F32),
        ),
        in_specs=[sm] * 4 + [vm] * 10,
        out_specs=(vm,) * 4,
        scratch_shapes=[
            pltpu.VMEM((288, 4, 128), F32),
            pltpu.VMEM((144, 8, 128), F32),
            pltpu.VMEM((288, 1, 128), F32),
            pltpu.VMEM((32, 128, 128), BF16),
            pltpu.VMEM((32, 128, 1024), BF16),
            pltpu.VMEM((32, 128, 1024), BF16),
            pltpu.VMEM((256, 8, 128), F32),
            pltpu.VMEM((32, 8, 128), F32),
            pltpu.VMEM((32, 8, 128), F32),
            pltpu.VMEM((1152, 128), jnp.int32),
            pltpu.VMEM((9, 8, 128), F32),
            pltpu.VMEM((512, 128), jnp.int32),
            pltpu.VMEM((1024, 128), F32),
            pltpu.VMEM((3, 3, 3, 16, 128), F32),
            pltpu.VMEM((2, 3, 3, 16, 128), F32),
            pltpu.VMEM((3, 3, 16, 128), F32),
            pltpu.VMEM((2, 3, 16, 128), F32),
            pltpu.VMEM((32, 128), jnp.int32),
            pltpu.VMEM((16, 128), jnp.int32),
            pltpu.VMEM((32, 128), F32),
            pltpu.VMEM((3, 32, 128), F32),
            pltpu.VMEM((3, 32, 128), F32),
            pltpu.VMEM((3, 16, 128), F32),
            pltpu.SemaphoreType.DMA((28,)),
            pltpu.SemaphoreType.DMA((28,)),
        ],
        compiler_params=pltpu.CompilerParams(
            collective_id=0, has_side_effects=True, vmem_limit_bytes=67043328
        ),
    )(
        fluid_lists.reshape(256),
        coupling_lists.reshape(128),
        fluid_counts.reshape(32),
        boulder_counts.reshape(16),
        fluid_position.reshape(3, 32, 128),
        fluid_velocity.reshape(3, 32, 128),
        fluid_mass.reshape(32, 128),
        coupling_lists.reshape(1, 128),
        boulder_position.reshape(3, 16, 128),
        boulder_velocity.reshape(3, 16, 128),
        boulder_radius.reshape(16, 128),
        boulder_mass.reshape(16, 128),
        contact_ids.reshape(8, 2048),
        spring_history.reshape(3, 8, 2048),
    )
    fa, fd, ba, ho = outs
    return (
        fa.reshape(3, 1, 1, 4096),
        fd.reshape(1, 1, 4096),
        ba.reshape(3, 1, 1, 2048),
        ho.reshape(3, 1, 1, 8, 2048),
    )


def solution(mesh):
    v4 = P(None, "gx", "gy", None)
    v3 = P("gx", "gy", None)
    l4 = P("gx", "gy", None, None)
    h5 = P(None, "gx", "gy", None, None)
    return jax.shard_map(
        body,
        mesh=mesh,
        in_specs=(v4, v4, v3, v3, l4, l4, v4, v4, v3, v3, v3, l4, h5),
        out_specs=(v4, v3, v4, h5),
        check_vma=False,
    )
```

```python
import jax
import jax.numpy as jnp
from jax import lax
from jax.experimental import pallas as pl
from jax.experimental.pallas import tpu as pltpu
from jax.sharding import PartitionSpec as P

F32 = jnp.float32
BF16 = jnp.bfloat16
MESH = pl.DeviceIdType.MESH
NT = (((1,), (1,)), ((), ()))
NN = (((1,), (0,)), ((), ()))

INV_H2 = 1.0 / 0.3**2
REST = 10.0
STIFF = 10.0
COUPLE = 0.1
NORMAL_K = 10.0
SHEAR_K = 20.0
DT = 0.05
SOFT2 = 0.02**2
PRESS_C = 6.0 / 0.3**2
X_UNIT = 2.0**21
V_HALF = 32766
R_LOW = 0.03
R_UNIT = ((1 << 17) - 4) / 0.04


def paired(lo, hi, one):
    def two(i, _):
        for k in range(4):
            one(4 * i + k, 0)
        return 0

    lax.fori_loop(lo // 4, hi // 4, two, 0)


def rounded(x):
    return x.astype(BF16).astype(F32)


def split3(x):
    hi = rounded(x)
    rest = x - hi
    mid = rounded(rest)
    return hi, mid, rest - mid


def dot(a, b, dims):
    return lax.dot_general(a, b, dims, preferred_element_type=F32)


def row8(x):
    return jnp.broadcast_to(x, (8, x.shape[-1]))


def halves(x):
    hi = x.astype(BF16)
    return hi, (x - hi.astype(F32)).astype(BF16)


def tile_offsets(tile):
    third = (tile * 11) >> 5
    return (third - 1).astype(F32), (tile - 3 * third - 1).astype(F32)


def kernel(
    fl, cl, fcnt, bcnt,
    fpos, fvel, fmass, clv, bpos, bvel, brad, bmass, cid, hist,
    o_fa, o_fd, o_ba, o_h,
    hf, hb, hd, ut, qh, ql, stg, tf, tb, gb, ft, fi, hp, sc, ga, sp, cp, ry, red, rx,
    cnf, cnb, dens, dr, pf, pu, ssem, rsem,
    *, n_x, n_y,
):
    me_x = lax.axis_index("gx")
    me_y = lax.axis_index("gy")
    xp = (lax.rem(me_x + 1, n_x), me_y)
    xm = (lax.rem(me_x + n_x - 1, n_x), me_y)
    yp = (me_x, lax.rem(me_y + 1, n_y))
    ym = (me_x, lax.rem(me_y + n_y - 1, n_y))

    barrier = pltpu.get_barrier_semaphore()
    for dev in (xp, xm, yp, ym):
        pl.semaphore_signal(barrier, inc=1, device_id=dev, device_id_type=MESH)

    row = lax.broadcasted_iota(jnp.int32, (8, 128), 0)
    lane = lax.broadcasted_iota(jnp.int32, (32, 128), 1)

    for b in range(32):
        cnf[b : b + 1, :] = jnp.full((1, 128), fcnt[b], jnp.int32)
    for b in range(16):
        cnb[b : b + 1, :] = jnp.full((1, 128), bcnt[b], jnp.int32)
    f_on = lane < cnf[...]
    b_on = lane[:16] < cnb[...]
    hf[4, 0] = jnp.where(f_on, jnp.exp(jnp.log(fmass[...]) * (1.0 / 3.0)), 0.0)
    hb[4, 0] = jnp.where(b_on, bmass[...], 0.0)
    for d in range(3):
        hf[4, 1 + d] = fpos[d]
        hb[4, 1 + d] = bpos[d]
        hb[4, 4 + d] = bvel[d]
    hb[4, 7] = brad[...]

    def copy(src, dst, k, dev):
        return pltpu.make_async_remote_copy(
            src_ref=src, dst_ref=dst, send_sem=ssem.at[k], recv_sem=rsem.at[k],
            device_id=dev, device_id_type=MESH,
        )

    def halo(ref, base):
        at = lambda t: ref.at[t]
        return {
            1: copy(at(4), at(1), base + 0, xp),
            7: copy(at(4), at(7), base + 1, xm),
            3: copy(at(4), at(3), base + 2, yp),
            5: copy(at(4), at(5), base + 3, ym),
            0: copy(at(1), at(0), base + 4, yp),
            2: copy(at(1), at(2), base + 5, ym),
            6: copy(at(7), at(6), base + 6, yp),
            8: copy(at(7), at(8), base + 7, ym),
        }

    cf = halo(hf, 0)
    cb = halo(hb, 8)
    cd = halo(hd, 16)
    c_yp = copy(cp.at[2], ry.at[0], 24, yp)
    c_ym = copy(cp.at[0], ry.at[1], 25, ym)
    c_xp = copy(red.at[2], rx.at[0], 26, xp)
    c_xm = copy(red.at[0], rx.at[1], 27, xm)

    one1 = jnp.ones((1, 128), F32)
    zeros = lambda n: jnp.zeros((n, 128), F32)

    def own_left(i, _):
        at = pl.ds(i, 1)
        x = [fpos[d, at, :] - 0.5 for d in range(3)]
        norm = -(x[0] * x[0] + x[1] * x[1] + x[2] * x[2])
        h, m, l = split3(jnp.concatenate([norm, x[0], x[1], x[2], one1, zeros(3)], axis=0))
        h, m, l = h[0:5], m[0:5], l[0:5]
        full = jnp.concatenate(
            [h, h, h, zeros(1), m, m, zeros(6), l, zeros(91)], axis=0
        )
        ut[i] = full.T.astype(BF16)
        return 0

    paired(0, 32, own_left)
    mf_live = jnp.where(f_on, fmass[...], 0.0)
    for r, v in enumerate([mf_live] + [mf_live * fvel[d] for d in range(3)]):
        hi = rounded(v)
        fi[pl.ds(r, 32, stride=8), :] = hi
        fi[pl.ds(4 + r, 32, stride=8), :] = v - hi

    pl.semaphore_wait(barrier, 4)
    for k in (1, 7, 3, 5):
        cf[k].start()
    for k in (1, 7, 3, 5):
        cb[k].start()

    def settle(dst, t, blocks):
        def four(g, _):
            for j in range(4):
                at = t * blocks + g * 4 + j
                dst[at] = stg[pl.ds(pl.multiple_of(at * 16, 16), 16), :].astype(BF16)
            return 0

        lax.fori_loop(0, blocks // 4, four, 0)

    def centred(ref, t):
        return [ref[t, 1] + (t // 3 - 1.5), ref[t, 2] + (t % 3 - 1.5), ref[t, 3] - 0.5]

    def pair_rows(t, blocks, c, x, scale):
        n = (x[0] * x[0] + x[1] * x[1]) + x[2] * x[2]
        cs = c * scale
        rows = [cs] + [(2.0 * cs) * v for v in x] + [c * (1.0 - scale * n)]
        for r, v in enumerate(rows):
            for k, part in enumerate(split3(v)):
                stg[pl.ds(t * blocks * 16 + 5 * k + r, blocks, stride=16), :] = part
        stg[pl.ds(t * blocks * 16 + 15, blocks, stride=16), :] = zeros(blocks)

    def fluid_table(t):
        pair_rows(t, 32, hf[t, 0], centred(hf, t), INV_H2)
        settle(tf, t, 32)

    def boulder_table(t):
        m = hb[t, 0]
        c = jnp.where(m > 0.0, jnp.sqrt(jnp.maximum(m, 1e-30)), 0.0)
        reach = hb[t, 7] + COUPLE
        pair_rows(t, 16, c, centred(hb, t), 1.0 / (reach * reach))
        settle(tb, t, 16)
        ones = jnp.ones((16, 128), F32)
        for r in range(4):
            v = ones if r == 0 else hb[t, 3 + r]
            hi = rounded(v)
            base = t * 256 + r
            stg[pl.ds(base, 16, stride=16), :] = hi
            stg[pl.ds(base + 4, 16, stride=16), :] = v - hi
        settle(gb, t, 16)

    def pack(t):
        plane = lambda f: hb[t, f]
        vel = [plane(4 + d) for d in range(3)]
        top = jnp.maximum(jnp.maximum(jnp.abs(vel[0]), jnp.abs(vel[1])), jnp.abs(vel[2]))
        top = jnp.max(jnp.max(top, axis=0, keepdims=True), axis=1, keepdims=True)
        top = jnp.maximum(jnp.broadcast_to(top, (8, 128)), 1e-30)
        sc[t] = top * (1.0 / V_HALF)
        inv = V_HALF / top[0:1]
        coord = [
            jnp.minimum((plane(1 + d) * X_UNIT).astype(jnp.int32), (1 << 21) - 1) for d in range(3)
        ]
        code = [(v * inv + (V_HALF + 1.5)).astype(jnp.int32) for v in vel]
        rad = (jnp.maximum(plane(7) - R_LOW, 0.0) * R_UNIT + 1.5).astype(jnp.int32)
        rad = jnp.where(plane(0) > 0.0, jnp.minimum(rad, (1 << 17) - 1), 0)
        words = [(coord[d] << 11) | (code[d] >> 5) for d in range(3)]
        words.append(
            (rad << 15) | ((code[0] & 31) << 10) | ((code[1] & 31) << 5) | (code[2] & 31)
        )
        for w in range(4):
            for half in range(2):
                hp[pl.ds(t * 128 + half * 4 + w, 16, stride=8), :] = words[w]

    def gather(tiles, first):
        for t in tiles:
            pack(t)

        def block(b, _):
            st = pl.multiple_of(b * 128, 128)
            ids8 = cid[:, pl.ds(st, 128)]
            for q in range(4):
                ids = jnp.where(row < 4, row8(ids8[2 * q : 2 * q + 1]), row8(ids8[2 * q + 1 : 2 * q + 2]))
                ln = ids & 127
                bits = [(ids & (128 << k)) != 0 for k in range(4)]
                tl = ids >> 11
                at = pl.ds(pl.multiple_of(b * 32 + q * 8, 8), 8)
                out = None if first else ga[at, :]
                for t in tiles:
                    vals = [
                        jnp.take_along_axis(
                            hp[(t * 16 + r) * 8 : (t * 16 + r + 1) * 8, :], ln, axis=1,
                            mode="promise_in_bounds",
                        )
                        for r in range(16)
                    ]
                    for k in range(4):
                        vals = [
                            jnp.where(bits[k], vals[j + 1], vals[j]) for j in range(0, len(vals), 2)
                        ]
                    out = vals[0] if out is None else jnp.where(tl == t, vals[0], out)
                ga[at, :] = out
            return 0

        lax.fori_loop(0, 16, block, 0)

    fluid_table(4)
    boulder_table(4)
    cf[3].wait_recv()
    cf[5].wait_recv()
    fluid_table(3)
    fluid_table(5)
    gather((4,), True)

    for k in (1, 7):
        cf[k].wait_recv()
    for k in (0, 2, 6, 8):
        cf[k].start()
    fluid_table(1)
    fluid_table(7)
    cb[3].wait_recv()
    cb[5].wait_recv()
    boulder_table(3)
    boulder_table(5)
    for k in (0, 2, 6, 8):
        cf[k].wait_recv()
        fluid_table(k)

    ones8 = jnp.ones((8, 128), BF16)

    def density(i, _):
        lhs = ut[i][:, 0:48]
        acc = jnp.zeros((128, 128), F32)
        for jj in range(4):
            t2 = jnp.concatenate([tf[fl[i * 8 + jj * 2]], tf[fl[i * 8 + jj * 2 + 1]]], axis=1)
            u = jnp.maximum(dot(lhs, jnp.concatenate([t2, t2, t2], axis=0), NN), 0.0)
            sq = u * u
            cube = sq * u
            acc = acc + (cube[:, 0:128] + cube[:, 128:256])
            at = slice(jj * 256, (jj + 1) * 256)
            qh[i, :, at] = sq.astype(BF16)
            ql[i, :, at] = (sq - qh[i, :, at].astype(F32)).astype(BF16)
        a, b, c = split3(acc)
        total = (
            dot(ones8, a.astype(BF16), NT)
            + dot(ones8, b.astype(BF16), NT)
            + dot(ones8, c.astype(BF16), NT)
        )
        dens[pl.ds(i, 1), :] = total[0:1]
        return 0

    paired(0, 16, density)
    for k in (1, 7):
        cb[k].wait_recv()
    for k in (0, 2, 6, 8):
        cb[k].start()
    paired(16, 32, density)
    rho = fmass[...] + dens[...]
    hd[4] = STIFF * (rho / REST - 1.0) / (rho * rho)
    for k in (1, 7, 3, 5):
        cd[k].start()
    o_fd[...] = jnp.where(f_on, rho, 0.0)

    boulder_table(1)
    boulder_table(7)
    for k in (0, 2, 6, 8):
        cb[k].wait_recv()
        boulder_table(k)

    def coupling(i, _):
        lhs = ut[i][:, 0:48]
        fside = fi[pl.ds(pl.multiple_of(i * 8, 8), 8), :].astype(BF16)
        pulled = jnp.zeros((16, 128), F32)
        for h in range(2):
            n0, n1 = cl[i * 4 + 2 * h], cl[i * 4 + 2 * h + 1]
            t2 = jnp.concatenate([tb[n0], tb[n1]], axis=1)
            u = jnp.maximum(dot(lhs, jnp.concatenate([t2, t2, t2], axis=0), NN), 0.0)
            hi, lo = halves(u * u)
            fun = jnp.concatenate([gb[n0], gb[n1]], axis=1)
            pulled = pulled + dot(fun, hi, NT) + dot(fun, lo, NT)
            back = dot(fside, hi, NN) + dot(fside, lo, NN)
            for g in range(2):
                at = pl.ds(pl.multiple_of((i * 4 + 2 * h + g) * 8, 8), 8)
                sp[at, :] = back[:, g * 128 : (g + 1) * 128]
        d4 = pulled[0:4] + pulled[4:8]
        for r in range(4):
            dr[r, pl.ds(i, 1), :] = d4[r : r + 1]
        return 0

    paired(0, 20, coupling)
    for k in (1, 7):
        cd[k].wait_recv()
    for k in (0, 2, 6, 8):
        cd[k].start()
    paired(20, 32, coupling)

    onehot = (
        lax.broadcasted_iota(jnp.int32, (144, 128), 0) == jnp.broadcast_to(clv[...], (144, 128))
    ).astype(F32).astype(BF16)

    def reduced(r):
        both = sp[pl.ds(r, 128, stride=8), :] + sp[pl.ds(r + 4, 128, stride=8), :]
        m = jnp.concatenate([v.astype(BF16) for v in split3(both)], axis=1)
        got = dot(onehot, m, NN)
        return got[:, 0:128] + got[:, 128:256] + got[:, 256:384]

    mass_sum = reduced(0)
    for d in range(3):
        pulls = reduced(1 + d)
        for t in range(9):
            at = slice(t * 16, (t + 1) * 16)
            cp[t % 3, t // 3, d] = pulls[at] - hb[t, 4 + d] * mass_sum[at]
    c_yp.start()
    c_ym.start()

    def press_table(t):
        c = hf[t, 0]
        rows = [c] + [c * v for v in centred(hf, t)]
        w = hd[t]
        rows = rows + [w * v for v in rows]
        for r, v in enumerate(rows):
            hi = rounded(v)
            base = t * 512 + r
            stg[pl.ds(base, 32, stride=16), :] = hi
            stg[pl.ds(base + 8, 32, stride=16), :] = v - hi
        settle(ft, t, 32)

    for k in (4, 1, 7):
        press_table(k)
    for k in (3, 5, 0, 2, 6, 8):
        cd[k].wait_recv()
        press_table(k)

    def pressure(i, _):
        fun = jnp.concatenate([ft[fl[i * 8 + j]] for j in range(8)], axis=1)
        got = dot(fun, qh[i], NT) + dot(fun, ql[i], NT)
        p8 = got[0:8] + got[8:16]
        at = pl.ds(i, 1)
        w_i = hd[4, at, :]
        comb = [w_i * p8[r : r + 1] + p8[4 + r : 5 + r] for r in range(4)]
        for d in range(3):
            pf[d, at, :] = (fpos[d, at, :] - 0.5) * comb[0] - comb[d + 1]
        return 0

    paired(0, 16, pressure)
    c_yp.wait_recv()
    c_ym.wait_recv()
    for g in range(3):
        red[g] = cp[1, g] + (ry[0, g] + ry[1, g])
    c_xp.start()
    c_xm.start()
    paired(16, 32, pressure)
    for d in range(3):
        down = -1.0 if d == 2 else 0.0
        drag = dr[1 + d] - fvel[d] * dr[0]
        o_fa[d] = jnp.where(f_on, PRESS_C * pf[d] + drag + down, 0.0)

    gather((3, 5, 1, 7), False)
    gather((0, 2, 6, 8), False)

    def contact(b, _):
        st = pl.multiple_of(b * 128, 128)
        ids = cid[:, pl.ds(st, 128)]
        tile = ids >> 11
        ox, oy = tile_offsets(tile)
        base = b * 32
        words = [ga[pl.ds(base + w, 8, stride=4), :] for w in range(4)]
        step = sc[0]
        for t in range(1, 9):
            step = jnp.where(tile == t, sc[t], step)
        low = words[3]
        xyz = [
            ((words[d] >> 11) & ((1 << 21) - 1)).astype(F32) * (1.0 / X_UNIT) + 0.5 / X_UNIT
            for d in range(3)
        ]
        pvel = [
            ((((words[d] & 2047) << 5) | ((low >> (10 - 5 * d)) & 31)) - (V_HALF + 1)).astype(F32)
            * step
            for d in range(3)
        ]
        code = (low >> 15) & ((1 << 17) - 1)
        prad = (code - 1).astype(F32) * (1.0 / R_UNIT) + R_LOW
        at = pl.ds(b, 1)
        r1 = row8(bpos[0, at, :]) - (xyz[0] + ox)
        r2 = row8(bpos[1, at, :]) - (xyz[1] + oy)
        r3 = row8(bpos[2, at, :]) - xyz[2]
        dist = jnp.sqrt((r1 * r1 + r2 * r2) + r3 * r3 + SOFT2)
        inv = 1.0 / dist
        nrm = (r1 * inv, r2 * inv, r3 * inv)
        inter = jnp.where(code > 0, jnp.maximum(row8(brad[at, :]) + prad - dist, 0.0), 0.0)
        rel = [row8(bvel[d, at, :]) - pvel[d] for d in range(3)]
        along = (rel[0] * nrm[0] + rel[1] * nrm[1]) + rel[2] * nrm[2]
        touch = jnp.minimum(inter * 100.0, 1.0)
        on = lax.broadcasted_iota(jnp.int32, (8, 128), 1) < jnp.broadcast_to(cnb[at, :], (8, 128))
        for d in range(3):
            spring = (hist[d, :, pl.ds(st, 128)] + DT * (rel[d] - along * nrm[d])) * touch
            push = NORMAL_K * inter * nrm[d] - SHEAR_K * spring
            pu[d, at, :] = jnp.sum(push, axis=0, keepdims=True)
            o_h[d, :, pl.ds(st, 128)] = jnp.where(on, spring, 0.0)
        return 0

    lax.fori_loop(0, 16, contact, 0)

    c_xp.wait_recv()
    c_xm.wait_recv()
    for d in range(3):
        down = -1.0 if d == 2 else 0.0
        coupled = red[1, d] + (rx[0, d] + rx[1, d])
        o_ba[d] = jnp.where(b_on, (pu[d] + coupled) / bmass[...] + down, 0.0)

    for group in (cf, cb, cd):
        for k in group:
            group[k].wait_send()
    for c in (c_yp, c_ym, c_xp, c_xm):
        c.wait_send()


def body(
    fluid_position, fluid_velocity, fluid_mass, fluid_counts, fluid_lists, coupling_lists,
    boulder_position, boulder_velocity, boulder_radius, boulder_mass, boulder_counts,
    contact_ids, spring_history,
):
    n_x, n_y = lax.axis_size("gx"), lax.axis_size("gy")
    vm = pl.BlockSpec(memory_space=pltpu.VMEM)
    sm = pl.BlockSpec(memory_space=pltpu.SMEM)
    outs = pl.pallas_call(
        lambda *refs: kernel(*refs, n_x=n_x, n_y=n_y),
        name="step",
        out_shape=(
            jax.ShapeDtypeStruct((3, 32, 128), F32),
            jax.ShapeDtypeStruct((32, 128), F32),
            jax.ShapeDtypeStruct((3, 16, 128), F32),
            jax.ShapeDtypeStruct((3, 8, 2048), F32),
        ),
        in_specs=[sm] * 4 + [vm] * 10,
        out_specs=(vm,) * 4,
        scratch_shapes=[
            pltpu.VMEM((9, 4, 32, 128), F32),
            pltpu.VMEM((9, 8, 16, 128), F32),
            pltpu.VMEM((9, 32, 128), F32),
            pltpu.VMEM((32, 128, 128), BF16),
            pltpu.VMEM((32, 128, 1024), BF16),
            pltpu.VMEM((32, 128, 1024), BF16),
            pltpu.VMEM((4608, 128), F32),
            pltpu.VMEM((288, 16, 128), BF16),
            pltpu.VMEM((144, 16, 128), BF16),
            pltpu.VMEM((144, 16, 128), BF16),
            pltpu.VMEM((288, 16, 128), BF16),
            pltpu.VMEM((256, 128), F32),
            pltpu.VMEM((1152, 128), jnp.int32),
            pltpu.VMEM((9, 8, 128), F32),
            pltpu.VMEM((512, 128), jnp.int32),
            pltpu.VMEM((1024, 128), F32),
            pltpu.VMEM((3, 3, 3, 16, 128), F32),
            pltpu.VMEM((2, 3, 3, 16, 128), F32),
            pltpu.VMEM((3, 3, 16, 128), F32),
            pltpu.VMEM((2, 3, 16, 128), F32),
            pltpu.VMEM((32, 128), jnp.int32),
            pltpu.VMEM((16, 128), jnp.int32),
            pltpu.VMEM((32, 128), F32),
            pltpu.VMEM((4, 32, 128), F32),
            pltpu.VMEM((3, 32, 128), F32),
            pltpu.VMEM((3, 16, 128), F32),
            pltpu.SemaphoreType.DMA((28,)),
            pltpu.SemaphoreType.DMA((28,)),
        ],
        compiler_params=pltpu.CompilerParams(
            collective_id=0, has_side_effects=True, vmem_limit_bytes=67043328
        ),
    )(
        fluid_lists.reshape(256),
        coupling_lists.reshape(128),
        fluid_counts.reshape(32),
        boulder_counts.reshape(16),
        fluid_position.reshape(3, 32, 128),
        fluid_velocity.reshape(3, 32, 128),
        fluid_mass.reshape(32, 128),
        coupling_lists.reshape(1, 128),
        boulder_position.reshape(3, 16, 128),
        boulder_velocity.reshape(3, 16, 128),
        boulder_radius.reshape(16, 128),
        boulder_mass.reshape(16, 128),
        contact_ids.reshape(8, 2048),
        spring_history.reshape(3, 8, 2048),
    )
    fa, fd, ba, ho = outs
    return (
        fa.reshape(3, 1, 1, 4096),
        fd.reshape(1, 1, 4096),
        ba.reshape(3, 1, 1, 2048),
        ho.reshape(3, 1, 1, 8, 2048),
    )


def solution(mesh):
    v4 = P(None, "gx", "gy", None)
    v3 = P("gx", "gy", None)
    l4 = P("gx", "gy", None, None)
    h5 = P(None, "gx", "gy", None, None)
    return jax.shard_map(
        body,
        mesh=mesh,
        in_specs=(v4, v4, v3, v3, l4, l4, v4, v4, v3, v3, v3, l4, h5),
        out_specs=(v4, v3, v4, h5),
        check_vma=False,
    )
```

```python
import jax
import jax.numpy as jnp
from jax import lax
from jax.experimental import pallas as pl
from jax.experimental.pallas import tpu as pltpu
from jax.sharding import PartitionSpec as P

F32 = jnp.float32
BF16 = jnp.bfloat16
MESH = pl.DeviceIdType.MESH
NT = (((1,), (1,)), ((), ()))
NN = (((1,), (0,)), ((), ()))

INV_H2 = 1.0 / 0.3**2
REST = 10.0
STIFF = 10.0
COUPLE = 0.1
NORMAL_K = 10.0
SHEAR_K = 20.0
DT = 0.05
SOFT2 = 0.02**2
PRESS_C = 6.0 / 0.3**2
X_UNIT = 2.0**21
V_HALF = 32766
R_LOW = 0.03
R_UNIT = ((1 << 17) - 4) / 0.04


def paired(lo, hi, one):
    def two(i, _):
        for k in range(4):
            one(4 * i + k, 0)
        return 0

    lax.fori_loop(lo // 4, hi // 4, two, 0)


def beside(lo, hi, one, extra):
    def step(b, _):
        for k in range(4):
            one(4 * b + k, 0)
        extra(2 * b, 0)
        extra(2 * b + 1, 0)
        return 0

    lax.fori_loop(lo // 2, hi // 2, step, 0)


def rounded(x):
    return x.astype(BF16).astype(F32)


def split3(x):
    hi = rounded(x)
    rest = x - hi
    mid = rounded(rest)
    return hi, mid, rest - mid


def dot(a, b, dims):
    return lax.dot_general(a, b, dims, preferred_element_type=F32)


def row8(x):
    return jnp.broadcast_to(x, (8, x.shape[-1]))


def halves(x):
    hi = x.astype(BF16)
    return hi, (x - hi.astype(F32)).astype(BF16)


def tile_offsets(tile):
    third = (tile * 11) >> 5
    return (third - 1).astype(F32), (tile - 3 * third - 1).astype(F32)


def kernel(
    fl, cl, fcnt, bcnt,
    fpos, fvel, fmass, bpos, bvel, brad, bmass, cid, hist,
    o_fa, o_fd, o_ba, o_h,
    hf, hb, hd, ut, qh, ql, stg, tf, tb, gb, ft, fi, hp, sc, ga, sp, cp, ry, red, rx,
    idc, cnf, cnb, dens, dr, pf, pu, ssem, rsem,
    *, n_x, n_y,
):
    me_x = lax.axis_index("gx")
    me_y = lax.axis_index("gy")
    xp = (lax.rem(me_x + 1, n_x), me_y)
    xm = (lax.rem(me_x + n_x - 1, n_x), me_y)
    yp = (me_x, lax.rem(me_y + 1, n_y))
    ym = (me_x, lax.rem(me_y + n_y - 1, n_y))

    barrier = pltpu.get_barrier_semaphore()
    for dev in (xp, xm, yp, ym):
        pl.semaphore_signal(barrier, inc=1, device_id=dev, device_id_type=MESH)

    row = lax.broadcasted_iota(jnp.int32, (8, 128), 0)
    lane = lax.broadcasted_iota(jnp.int32, (32, 128), 1)

    for b in range(32):
        cnf[b : b + 1, :] = jnp.full((1, 128), fcnt[0, 0, b], jnp.int32)
    for b in range(16):
        cnb[b : b + 1, :] = jnp.full((1, 128), bcnt[0, 0, b], jnp.int32)
    f_on = lane < cnf[...]
    b_on = lane[:16] < cnb[...]
    hf[4, 0] = jnp.where(f_on, jnp.exp(jnp.log(fmass[...]) * (1.0 / 3.0)), 0.0)
    hb[4, 0] = jnp.where(b_on, bmass[...], 0.0)
    for d in range(3):
        hf[4, 1 + d] = fpos[d]
        hb[4, 1 + d] = bpos[d]
        hb[4, 4 + d] = bvel[d]
    hb[4, 7] = brad[...]

    def copy(src, dst, k, dev):
        return pltpu.make_async_remote_copy(
            src_ref=src, dst_ref=dst, send_sem=ssem.at[k], recv_sem=rsem.at[k],
            device_id=dev, device_id_type=MESH,
        )

    def halo(ref, base):
        at = lambda t: ref.at[t]
        return {
            1: copy(at(4), at(1), base + 0, xp),
            7: copy(at(4), at(7), base + 1, xm),
            3: copy(at(4), at(3), base + 2, yp),
            5: copy(at(4), at(5), base + 3, ym),
            0: copy(at(1), at(0), base + 4, yp),
            2: copy(at(1), at(2), base + 5, ym),
            6: copy(at(7), at(6), base + 6, yp),
            8: copy(at(7), at(8), base + 7, ym),
        }

    cf = halo(hf, 0)
    cb = halo(hb, 8)
    cd = halo(hd, 16)
    c_yp = copy(cp.at[2], ry.at[0], 24, yp)
    c_ym = copy(cp.at[0], ry.at[1], 25, ym)
    c_xp = copy(red.at[2], rx.at[0], 26, xp)
    c_xm = copy(red.at[0], rx.at[1], 27, xm)

    for e in range(128):
        idc[e : e + 1, :] = jnp.full((1, 128), cl[0, 0, e // 4, e % 4], jnp.int32)

    one1 = jnp.ones((1, 128), F32)
    zeros = lambda n: jnp.zeros((n, 128), F32)

    def own_left(i, _):
        at = pl.ds(i, 1)
        x = [fpos[d, at, :] - 0.5 for d in range(3)]
        norm = -(x[0] * x[0] + x[1] * x[1] + x[2] * x[2])
        h, m, l = split3(jnp.concatenate([norm, x[0], x[1], x[2], one1, zeros(3)], axis=0))
        h, m, l = h[0:5], m[0:5], l[0:5]
        full = jnp.concatenate(
            [h, h, h, zeros(1), m, m, zeros(6), l, zeros(91)], axis=0
        )
        ut[i] = full.T.astype(BF16)
        return 0

    paired(0, 32, own_left)
    mf_live = jnp.where(f_on, fmass[...], 0.0)
    for r, v in enumerate([mf_live] + [mf_live * fvel[d] for d in range(3)]):
        hi = rounded(v)
        fi[pl.ds(r, 32, stride=8), :] = hi
        fi[pl.ds(4 + r, 32, stride=8), :] = v - hi

    pl.semaphore_wait(barrier, 4)
    for k in (1, 7, 3, 5):
        cf[k].start()
    for k in (1, 7, 3, 5):
        cb[k].start()

    def settle(dst, t, blocks):
        def four(g, _):
            for j in range(4):
                at = t * blocks + g * 4 + j
                dst[at] = stg[pl.ds(pl.multiple_of(at * 16, 16), 16), :].astype(BF16)
            return 0

        lax.fori_loop(0, blocks // 4, four, 0)

    def centred(ref, t):
        return [ref[t, 1] + (t // 3 - 1.5), ref[t, 2] + (t % 3 - 1.5), ref[t, 3] - 0.5]

    def pair_rows(t, blocks, c, x, scale):
        n = (x[0] * x[0] + x[1] * x[1]) + x[2] * x[2]
        cs = c * scale
        rows = [cs] + [(2.0 * cs) * v for v in x] + [c * (1.0 - scale * n)]
        for r, v in enumerate(rows):
            for k, part in enumerate(split3(v)):
                stg[pl.ds(t * blocks * 16 + 5 * k + r, blocks, stride=16), :] = part
        stg[pl.ds(t * blocks * 16 + 15, blocks, stride=16), :] = zeros(blocks)

    def fluid_table(t):
        pair_rows(t, 32, hf[t, 0], centred(hf, t), INV_H2)
        settle(tf, t, 32)

    def boulder_table(t):
        m = hb[t, 0]
        c = jnp.where(m > 0.0, jnp.sqrt(jnp.maximum(m, 1e-30)), 0.0)
        reach = hb[t, 7] + COUPLE
        pair_rows(t, 16, c, centred(hb, t), 1.0 / (reach * reach))
        settle(tb, t, 16)
        ones = jnp.ones((16, 128), F32)
        for r in range(4):
            v = ones if r == 0 else hb[t, 3 + r]
            hi = rounded(v)
            base = t * 256 + r
            stg[pl.ds(base, 16, stride=16), :] = hi
            stg[pl.ds(base + 4, 16, stride=16), :] = v - hi
        settle(gb, t, 16)

    def pack(t):
        plane = lambda f: hb[t, f]
        vel = [plane(4 + d) for d in range(3)]
        top = jnp.maximum(jnp.maximum(jnp.abs(vel[0]), jnp.abs(vel[1])), jnp.abs(vel[2]))
        top = jnp.max(jnp.max(top, axis=0, keepdims=True), axis=1, keepdims=True)
        top = jnp.maximum(jnp.broadcast_to(top, (8, 128)), 1e-30)
        sc[t] = top * (1.0 / V_HALF)
        inv = V_HALF / top[0:1]
        coord = [
            jnp.minimum((plane(1 + d) * X_UNIT).astype(jnp.int32), (1 << 21) - 1) for d in range(3)
        ]
        code = [(v * inv + (V_HALF + 1.5)).astype(jnp.int32) for v in vel]
        rad = (jnp.maximum(plane(7) - R_LOW, 0.0) * R_UNIT + 1.5).astype(jnp.int32)
        rad = jnp.where(plane(0) > 0.0, jnp.minimum(rad, (1 << 17) - 1), 0)
        words = [(coord[d] << 11) | (code[d] >> 5) for d in range(3)]
        words.append(
            (rad << 15) | ((code[0] & 31) << 10) | ((code[1] & 31) << 5) | (code[2] & 31)
        )
        for w in range(4):
            for half in range(2):
                hp[pl.ds(t * 128 + half * 4 + w, 16, stride=8), :] = words[w]

    def gather(tiles, first):
        def block(b, _):
            st = pl.multiple_of(b * 128, 128)
            ids8 = cid[:, pl.ds(st, 128)]
            for q in range(4):
                ids = jnp.where(row < 4, row8(ids8[2 * q : 2 * q + 1]), row8(ids8[2 * q + 1 : 2 * q + 2]))
                ln = ids & 127
                bits = [(ids & (128 << k)) != 0 for k in range(4)]
                tl = ids >> 11
                at = pl.ds(pl.multiple_of(b * 32 + q * 8, 8), 8)
                out = None if first else ga[at, :]
                for t in tiles:
                    vals = [
                        jnp.take_along_axis(
                            hp[(t * 16 + r) * 8 : (t * 16 + r + 1) * 8, :], ln, axis=1,
                            mode="promise_in_bounds",
                        )
                        for r in range(16)
                    ]
                    for k in range(4):
                        vals = [
                            jnp.where(bits[k], vals[j + 1], vals[j]) for j in range(0, len(vals), 2)
                        ]
                    out = vals[0] if out is None else jnp.where(tl == t, vals[0], out)
                ga[at, :] = out
            return 0

        return block

    fluid_table(4)
    boulder_table(4)
    cf[3].wait_recv()
    cf[5].wait_recv()
    fluid_table(3)
    fluid_table(5)
    pack(4)
    lax.fori_loop(0, 16, gather((4,), True), 0)

    for k in (1, 7):
        cf[k].wait_recv()
    for k in (0, 2, 6, 8):
        cf[k].start()
    fluid_table(1)
    fluid_table(7)
    cb[3].wait_recv()
    cb[5].wait_recv()
    boulder_table(3)
    boulder_table(5)
    for k in (0, 2, 6, 8):
        cf[k].wait_recv()
        fluid_table(k)

    ones8 = jnp.ones((8, 128), BF16)

    def density(i, _):
        lhs = ut[i][:, 0:48]
        acc = jnp.zeros((128, 128), F32)
        for jj in range(4):
            t2 = jnp.concatenate([tf[fl[0, 0, i, jj * 2]], tf[fl[0, 0, i, jj * 2 + 1]]], axis=1)
            u = jnp.maximum(dot(lhs, jnp.concatenate([t2, t2, t2], axis=0), NN), 0.0)
            sq = u * u
            cube = sq * u
            acc = acc + (cube[:, 0:128] + cube[:, 128:256])
            at = slice(jj * 256, (jj + 1) * 256)
            qh[i, :, at] = sq.astype(BF16)
            ql[i, :, at] = (sq - qh[i, :, at].astype(F32)).astype(BF16)
        a, b, c = split3(acc)
        total = (
            dot(ones8, a.astype(BF16), NT)
            + dot(ones8, b.astype(BF16), NT)
            + dot(ones8, c.astype(BF16), NT)
        )
        dens[pl.ds(i, 1), :] = total[0:1]
        return 0

    pack(3)
    pack(5)
    side = gather((3, 5), False)
    beside(0, 8, density, side)
    for k in (1, 7):
        cb[k].wait_recv()
    for k in (0, 2, 6, 8):
        cb[k].start()
    beside(8, 16, density, side)
    rho = fmass[...] + dens[...]
    hd[4] = STIFF * (rho / REST - 1.0) / (rho * rho)
    for k in (1, 7, 3, 5):
        cd[k].start()
    o_fd[...] = jnp.where(f_on, rho, 0.0)

    boulder_table(1)
    boulder_table(7)
    for k in (0, 2, 6, 8):
        cb[k].wait_recv()
        boulder_table(k)

    def coupling(i, _):
        lhs = ut[i][:, 0:48]
        fside = fi[pl.ds(pl.multiple_of(i * 8, 8), 8), :].astype(BF16)
        pulled = jnp.zeros((16, 128), F32)
        for h in range(2):
            n0, n1 = cl[0, 0, i, 2 * h], cl[0, 0, i, 2 * h + 1]
            t2 = jnp.concatenate([tb[n0], tb[n1]], axis=1)
            u = jnp.maximum(dot(lhs, jnp.concatenate([t2, t2, t2], axis=0), NN), 0.0)
            hi, lo = halves(u * u)
            fun = jnp.concatenate([gb[n0], gb[n1]], axis=1)
            pulled = pulled + dot(fun, hi, NT) + dot(fun, lo, NT)
            back = dot(fside, hi, NN) + dot(fside, lo, NN)
            for g in range(2):
                at = pl.ds(pl.multiple_of((i * 4 + 2 * h + g) * 8, 8), 8)
                sp[at, :] = back[:, g * 128 : (g + 1) * 128]
        d4 = pulled[0:4] + pulled[4:8]
        for r in range(4):
            dr[r, pl.ds(i, 1), :] = d4[r : r + 1]
        return 0

    for t in (1, 7, 0, 2, 6, 8):
        pack(t)
    side = gather((1, 7, 0), False)
    beside(0, 10, coupling, side)
    for k in (1, 7):
        cd[k].wait_recv()
    for k in (0, 2, 6, 8):
        cd[k].start()
    beside(10, 16, coupling, side)

    onehot = (
        lax.broadcasted_iota(jnp.int32, (144, 128), 0)
        == jnp.broadcast_to(idc[...].T[0:1], (144, 128))
    ).astype(F32).astype(BF16)

    def reduced(r):
        both = sp[pl.ds(r, 128, stride=8), :] + sp[pl.ds(r + 4, 128, stride=8), :]
        m = jnp.concatenate([v.astype(BF16) for v in split3(both)], axis=1)
        got = dot(onehot, m, NN)
        return got[:, 0:128] + got[:, 128:256] + got[:, 256:384]

    mass_sum = reduced(0)
    for d in range(3):
        pulls = reduced(1 + d)
        for t in range(9):
            at = slice(t * 16, (t + 1) * 16)
            cp[t % 3, t // 3, d] = pulls[at] - hb[t, 4 + d] * mass_sum[at]
    c_yp.start()
    c_ym.start()

    def press_table(t):
        c = hf[t, 0]
        rows = [c] + [c * v for v in centred(hf, t)]
        w = hd[t]
        rows = rows + [w * v for v in rows]
        for r, v in enumerate(rows):
            hi = rounded(v)
            base = t * 512 + r
            stg[pl.ds(base, 32, stride=16), :] = hi
            stg[pl.ds(base + 8, 32, stride=16), :] = v - hi
        settle(ft, t, 32)

    for k in (4, 1, 7):
        press_table(k)
    for k in (3, 5, 0, 2, 6, 8):
        cd[k].wait_recv()
        press_table(k)

    def pressure(i, _):
        fun = jnp.concatenate([ft[fl[0, 0, i, j]] for j in range(8)], axis=1)
        got = dot(fun, qh[i], NT) + dot(fun, ql[i], NT)
        p8 = got[0:8] + got[8:16]
        at = pl.ds(i, 1)
        w_i = hd[4, at, :]
        comb = [w_i * p8[r : r + 1] + p8[4 + r : 5 + r] for r in range(4)]
        for d in range(3):
            pf[d, at, :] = (fpos[d, at, :] - 0.5) * comb[0] - comb[d + 1]
        return 0

    side = gather((2, 6, 8), False)
    beside(0, 8, pressure, side)
    c_yp.wait_recv()
    c_ym.wait_recv()
    for g in range(3):
        red[g] = cp[1, g] + (ry[0, g] + ry[1, g])
    c_xp.start()
    c_xm.start()
    beside(8, 16, pressure, side)
    for d in range(3):
        down = -1.0 if d == 2 else 0.0
        drag = dr[1 + d] - fvel[d] * dr[0]
        o_fa[d] = jnp.where(f_on, PRESS_C * pf[d] + drag + down, 0.0)

    def contact(b, _):
        st = pl.multiple_of(b * 128, 128)
        ids = cid[:, pl.ds(st, 128)]
        tile = ids >> 11
        ox, oy = tile_offsets(tile)
        base = b * 32
        words = [ga[pl.ds(base + w, 8, stride=4), :] for w in range(4)]
        step = sc[0]
        for t in range(1, 9):
            step = jnp.where(tile == t, sc[t], step)
        low = words[3]
        xyz = [
            ((words[d] >> 11) & ((1 << 21) - 1)).astype(F32) * (1.0 / X_UNIT) + 0.5 / X_UNIT
            for d in range(3)
        ]
        pvel = [
            ((((words[d] & 2047) << 5) | ((low >> (10 - 5 * d)) & 31)) - (V_HALF + 1)).astype(F32)
            * step
            for d in range(3)
        ]
        code = (low >> 15) & ((1 << 17) - 1)
        prad = (code - 1).astype(F32) * (1.0 / R_UNIT) + R_LOW
        at = pl.ds(b, 1)
        r1 = row8(bpos[0, at, :]) - (xyz[0] + ox)
        r2 = row8(bpos[1, at, :]) - (xyz[1] + oy)
        r3 = row8(bpos[2, at, :]) - xyz[2]
        dist = jnp.sqrt((r1 * r1 + r2 * r2) + r3 * r3 + SOFT2)
        inv = 1.0 / dist
        nrm = (r1 * inv, r2 * inv, r3 * inv)
        inter = jnp.where(code > 0, jnp.maximum(row8(brad[at, :]) + prad - dist, 0.0), 0.0)
        rel = [row8(bvel[d, at, :]) - pvel[d] for d in range(3)]
        along = (rel[0] * nrm[0] + rel[1] * nrm[1]) + rel[2] * nrm[2]
        touch = jnp.minimum(inter * 100.0, 1.0)
        on = lax.broadcasted_iota(jnp.int32, (8, 128), 1) < jnp.broadcast_to(cnb[at, :], (8, 128))
        for d in range(3):
            spring = (hist[d, :, pl.ds(st, 128)] + DT * (rel[d] - along * nrm[d])) * touch
            push = NORMAL_K * inter * nrm[d] - SHEAR_K * spring
            pu[d, at, :] = jnp.sum(push, axis=0, keepdims=True)
            o_h[d, :, pl.ds(st, 128)] = jnp.where(on, spring, 0.0)
        return 0

    lax.fori_loop(0, 16, contact, 0)

    c_xp.wait_recv()
    c_xm.wait_recv()
    for d in range(3):
        down = -1.0 if d == 2 else 0.0
        coupled = red[1, d] + (rx[0, d] + rx[1, d])
        o_ba[d] = jnp.where(b_on, (pu[d] + coupled) / bmass[...] + down, 0.0)

    for group in (cf, cb, cd):
        for k in group:
            group[k].wait_send()
    for c in (c_yp, c_ym, c_xp, c_xm):
        c.wait_send()


def body(
    fluid_position, fluid_velocity, fluid_mass, fluid_counts, fluid_lists, coupling_lists,
    boulder_position, boulder_velocity, boulder_radius, boulder_mass, boulder_counts,
    contact_ids, spring_history,
):
    n_x, n_y = lax.axis_size("gx"), lax.axis_size("gy")
    vm = pl.BlockSpec(memory_space=pltpu.VMEM)
    sm = pl.BlockSpec(memory_space=pltpu.SMEM)
    outs = pl.pallas_call(
        lambda *refs: kernel(*refs, n_x=n_x, n_y=n_y),
        name="step",
        out_shape=(
            jax.ShapeDtypeStruct((3, 32, 128), F32),
            jax.ShapeDtypeStruct((32, 128), F32),
            jax.ShapeDtypeStruct((3, 16, 128), F32),
            jax.ShapeDtypeStruct((3, 8, 2048), F32),
        ),
        in_specs=[sm] * 4 + [vm] * 9,
        out_specs=(vm,) * 4,
        scratch_shapes=[
            pltpu.VMEM((9, 4, 32, 128), F32),
            pltpu.VMEM((9, 8, 16, 128), F32),
            pltpu.VMEM((9, 32, 128), F32),
            pltpu.VMEM((32, 128, 128), BF16),
            pltpu.VMEM((32, 128, 1024), BF16),
            pltpu.VMEM((32, 128, 1024), BF16),
            pltpu.VMEM((4608, 128), F32),
            pltpu.VMEM((288, 16, 128), BF16),
            pltpu.VMEM((144, 16, 128), BF16),
            pltpu.VMEM((144, 16, 128), BF16),
            pltpu.VMEM((288, 16, 128), BF16),
            pltpu.VMEM((256, 128), F32),
            pltpu.VMEM((1152, 128), jnp.int32),
            pltpu.VMEM((9, 8, 128), F32),
            pltpu.VMEM((512, 128), jnp.int32),
            pltpu.VMEM((1024, 128), F32),
            pltpu.VMEM((3, 3, 3, 16, 128), F32),
            pltpu.VMEM((2, 3, 3, 16, 128), F32),
            pltpu.VMEM((3, 3, 16, 128), F32),
            pltpu.VMEM((2, 3, 16, 128), F32),
            pltpu.VMEM((128, 128), jnp.int32),
            pltpu.VMEM((32, 128), jnp.int32),
            pltpu.VMEM((16, 128), jnp.int32),
            pltpu.VMEM((32, 128), F32),
            pltpu.VMEM((4, 32, 128), F32),
            pltpu.VMEM((3, 32, 128), F32),
            pltpu.VMEM((3, 16, 128), F32),
            pltpu.SemaphoreType.DMA((28,)),
            pltpu.SemaphoreType.DMA((28,)),
        ],
        compiler_params=pltpu.CompilerParams(
            collective_id=0, has_side_effects=True, vmem_limit_bytes=67043328
        ),
    )(
        fluid_lists,
        coupling_lists,
        fluid_counts,
        boulder_counts,
        fluid_position.reshape(3, 32, 128),
        fluid_velocity.reshape(3, 32, 128),
        fluid_mass.reshape(32, 128),
        boulder_position.reshape(3, 16, 128),
        boulder_velocity.reshape(3, 16, 128),
        boulder_radius.reshape(16, 128),
        boulder_mass.reshape(16, 128),
        contact_ids.reshape(8, 2048),
        spring_history.reshape(3, 8, 2048),
    )
    fa, fd, ba, ho = outs
    return (
        fa.reshape(3, 1, 1, 4096),
        fd.reshape(1, 1, 4096),
        ba.reshape(3, 1, 1, 2048),
        ho.reshape(3, 1, 1, 8, 2048),
    )


def solution(mesh):
    v4 = P(None, "gx", "gy", None)
    v3 = P("gx", "gy", None)
    l4 = P("gx", "gy", None, None)
    h5 = P(None, "gx", "gy", None, None)
    return jax.shard_map(
        body,
        mesh=mesh,
        in_specs=(v4, v4, v3, v3, l4, l4, v4, v4, v3, v3, v3, l4, h5),
        out_specs=(v4, v3, v4, h5),
        check_vma=False,
    )
```

```python
import jax
import jax.numpy as jnp
from jax import lax
from jax.experimental import pallas as pl
from jax.experimental.pallas import tpu as pltpu
from jax.sharding import PartitionSpec as P

F32 = jnp.float32
BF16 = jnp.bfloat16
MESH = pl.DeviceIdType.MESH
NT = (((1,), (1,)), ((), ()))
NN = (((1,), (0,)), ((), ()))

INV_H2 = 1.0 / 0.3**2
REST = 10.0
STIFF = 10.0
COUPLE = 0.1
NORMAL_K = 10.0
SHEAR_K = 20.0
DT = 0.05
SOFT2 = 0.02**2
PRESS_C = 6.0 / 0.3**2
X_UNIT = 2.0**21
V_HALF = 32766
R_LOW = 0.03
R_UNIT = ((1 << 17) - 4) / 0.04


def paired(lo, hi, one):
    def two(i, _):
        for k in range(4):
            one(4 * i + k, 0)
        return 0

    lax.fori_loop(lo // 4, hi // 4, two, 0)


def beside(lo, hi, one, extra):
    def step(b, _):
        for k in range(4):
            one(4 * b + k, 0)
        extra(2 * b, 0)
        extra(2 * b + 1, 0)
        return 0

    lax.fori_loop(lo // 2, hi // 2, step, 0)


def rounded(x):
    return x.astype(BF16).astype(F32)


def split3(x):
    hi = rounded(x)
    rest = x - hi
    mid = rounded(rest)
    return hi, mid, rest - mid


def dot(a, b, dims):
    return lax.dot_general(a, b, dims, preferred_element_type=F32)


def row8(x):
    return jnp.broadcast_to(x, (8, x.shape[-1]))


def halves(x):
    hi = x.astype(BF16)
    return hi, (x - hi.astype(F32)).astype(BF16)


def tile_offsets(tile):
    third = (tile * 11) >> 5
    return (third - 1).astype(F32), (tile - 3 * third - 1).astype(F32)


def kernel(
    fl, cl, fcnt, bcnt,
    fpos, fvel, fmass, bpos, bvel, brad, bmass, cid,
    o_fa, o_fd, ga, sc, o_cp,
    hf, hb, hd, ut, qh, ql, stg, tf, tb, gb, ft, fi, hp, sp, cp, ry, red, rx,
    idc, cnf, cnb, dens, dr, pf, ssem, rsem,
    *, n_x, n_y,
):
    me_x = lax.axis_index("gx")
    me_y = lax.axis_index("gy")
    xp = (lax.rem(me_x + 1, n_x), me_y)
    xm = (lax.rem(me_x + n_x - 1, n_x), me_y)
    yp = (me_x, lax.rem(me_y + 1, n_y))
    ym = (me_x, lax.rem(me_y + n_y - 1, n_y))

    barrier = pltpu.get_barrier_semaphore()
    for dev in (xp, xm, yp, ym):
        pl.semaphore_signal(barrier, inc=1, device_id=dev, device_id_type=MESH)

    row = lax.broadcasted_iota(jnp.int32, (8, 128), 0)
    lane = lax.broadcasted_iota(jnp.int32, (32, 128), 1)

    for b in range(32):
        cnf[b : b + 1, :] = jnp.full((1, 128), fcnt[0, 0, b], jnp.int32)
    for b in range(16):
        cnb[b : b + 1, :] = jnp.full((1, 128), bcnt[0, 0, b], jnp.int32)
    f_on = lane < cnf[...]
    b_on = lane[:16] < cnb[...]
    hf[4, 0] = jnp.where(f_on, jnp.exp(jnp.log(fmass[...]) * (1.0 / 3.0)), 0.0)
    hb[4, 0] = jnp.where(b_on, bmass[...], 0.0)
    for d in range(3):
        hf[4, 1 + d] = fpos[d]
        hb[4, 1 + d] = bpos[d]
        hb[4, 4 + d] = bvel[d]
    hb[4, 7] = brad[...]

    def copy(src, dst, k, dev):
        return pltpu.make_async_remote_copy(
            src_ref=src, dst_ref=dst, send_sem=ssem.at[k], recv_sem=rsem.at[k],
            device_id=dev, device_id_type=MESH,
        )

    def halo(ref, base):
        at = lambda t: ref.at[t]
        return {
            1: copy(at(4), at(1), base + 0, xp),
            7: copy(at(4), at(7), base + 1, xm),
            3: copy(at(4), at(3), base + 2, yp),
            5: copy(at(4), at(5), base + 3, ym),
            0: copy(at(1), at(0), base + 4, yp),
            2: copy(at(1), at(2), base + 5, ym),
            6: copy(at(7), at(6), base + 6, yp),
            8: copy(at(7), at(8), base + 7, ym),
        }

    cf = halo(hf, 0)
    cb = halo(hb, 8)
    cd = halo(hd, 16)
    c_yp = copy(cp.at[2], ry.at[0], 24, yp)
    c_ym = copy(cp.at[0], ry.at[1], 25, ym)
    c_xp = copy(red.at[2], rx.at[0], 26, xp)
    c_xm = copy(red.at[0], rx.at[1], 27, xm)

    for e in range(128):
        idc[e : e + 1, :] = jnp.full((1, 128), cl[0, 0, e // 4, e % 4], jnp.int32)

    one1 = jnp.ones((1, 128), F32)
    zeros = lambda n: jnp.zeros((n, 128), F32)

    def own_left(i, _):
        at = pl.ds(i, 1)
        x = [fpos[d, at, :] - 0.5 for d in range(3)]
        norm = -(x[0] * x[0] + x[1] * x[1] + x[2] * x[2])
        h, m, l = split3(jnp.concatenate([norm, x[0], x[1], x[2], one1, zeros(3)], axis=0))
        h, m, l = h[0:5], m[0:5], l[0:5]
        full = jnp.concatenate(
            [h, h, h, zeros(1), m, m, zeros(6), l, zeros(91)], axis=0
        )
        ut[i] = full.T.astype(BF16)
        return 0

    paired(0, 32, own_left)
    mf_live = jnp.where(f_on, fmass[...], 0.0)
    for r, v in enumerate([mf_live] + [mf_live * fvel[d] for d in range(3)]):
        hi = rounded(v)
        fi[pl.ds(r, 32, stride=8), :] = hi
        fi[pl.ds(4 + r, 32, stride=8), :] = v - hi

    pl.semaphore_wait(barrier, 4)
    for k in (1, 7, 3, 5):
        cf[k].start()
    for k in (1, 7, 3, 5):
        cb[k].start()

    def settle(dst, t, blocks):
        def four(g, _):
            for j in range(4):
                at = t * blocks + g * 4 + j
                dst[at] = stg[pl.ds(pl.multiple_of(at * 16, 16), 16), :].astype(BF16)
            return 0

        lax.fori_loop(0, blocks // 4, four, 0)

    def centred(ref, t):
        return [ref[t, 1] + (t // 3 - 1.5), ref[t, 2] + (t % 3 - 1.5), ref[t, 3] - 0.5]

    def pair_rows(t, blocks, c, x, scale):
        n = (x[0] * x[0] + x[1] * x[1]) + x[2] * x[2]
        cs = c * scale
        rows = [cs] + [(2.0 * cs) * v for v in x] + [c * (1.0 - scale * n)]
        for r, v in enumerate(rows):
            for k, part in enumerate(split3(v)):
                stg[pl.ds(t * blocks * 16 + 5 * k + r, blocks, stride=16), :] = part
        stg[pl.ds(t * blocks * 16 + 15, blocks, stride=16), :] = zeros(blocks)

    def fluid_table(t):
        pair_rows(t, 32, hf[t, 0], centred(hf, t), INV_H2)
        settle(tf, t, 32)

    def boulder_table(t):
        m = hb[t, 0]
        c = jnp.where(m > 0.0, jnp.sqrt(jnp.maximum(m, 1e-30)), 0.0)
        reach = hb[t, 7] + COUPLE
        pair_rows(t, 16, c, centred(hb, t), 1.0 / (reach * reach))
        settle(tb, t, 16)
        ones = jnp.ones((16, 128), F32)
        for r in range(4):
            v = ones if r == 0 else hb[t, 3 + r]
            hi = rounded(v)
            base = t * 256 + r
            stg[pl.ds(base, 16, stride=16), :] = hi
            stg[pl.ds(base + 4, 16, stride=16), :] = v - hi
        settle(gb, t, 16)

    def pack(t):
        plane = lambda f: hb[t, f]
        vel = [plane(4 + d) for d in range(3)]
        top = jnp.maximum(jnp.maximum(jnp.abs(vel[0]), jnp.abs(vel[1])), jnp.abs(vel[2]))
        top = jnp.max(jnp.max(top, axis=0, keepdims=True), axis=1, keepdims=True)
        top = jnp.maximum(jnp.broadcast_to(top, (8, 128)), 1e-30)
        sc[t] = top * (1.0 / V_HALF)
        inv = V_HALF / top[0:1]
        coord = [
            jnp.minimum((plane(1 + d) * X_UNIT).astype(jnp.int32), (1 << 21) - 1) for d in range(3)
        ]
        code = [(v * inv + (V_HALF + 1.5)).astype(jnp.int32) for v in vel]
        rad = (jnp.maximum(plane(7) - R_LOW, 0.0) * R_UNIT + 1.5).astype(jnp.int32)
        rad = jnp.where(plane(0) > 0.0, jnp.minimum(rad, (1 << 17) - 1), 0)
        words = [(coord[d] << 11) | (code[d] >> 5) for d in range(3)]
        words.append(
            (rad << 15) | ((code[0] & 31) << 10) | ((code[1] & 31) << 5) | (code[2] & 31)
        )
        for w in range(4):
            for half in range(2):
                hp[pl.ds(t * 128 + half * 4 + w, 16, stride=8), :] = words[w]

    def gather(tiles, first):
        def block(b, _):
            st = pl.multiple_of(b * 128, 128)
            ids8 = cid[:, pl.ds(st, 128)]
            for q in range(4):
                ids = jnp.where(row < 4, row8(ids8[2 * q : 2 * q + 1]), row8(ids8[2 * q + 1 : 2 * q + 2]))
                ln = ids & 127
                bits = [(ids & (128 << k)) != 0 for k in range(4)]
                tl = ids >> 11
                at = pl.ds(pl.multiple_of(b * 32 + q * 8, 8), 8)
                out = None if first else ga[at, :]
                for t in tiles:
                    vals = [
                        jnp.take_along_axis(
                            hp[(t * 16 + r) * 8 : (t * 16 + r + 1) * 8, :], ln, axis=1,
                            mode="promise_in_bounds",
                        )
                        for r in range(16)
                    ]
                    for k in range(4):
                        vals = [
                            jnp.where(bits[k], vals[j + 1], vals[j]) for j in range(0, len(vals), 2)
                        ]
                    out = vals[0] if out is None else jnp.where(tl == t, vals[0], out)
                ga[at, :] = out
            return 0

        return block

    fluid_table(4)
    boulder_table(4)
    cf[3].wait_recv()
    cf[5].wait_recv()
    fluid_table(3)
    fluid_table(5)
    pack(4)
    lax.fori_loop(0, 16, gather((4,), True), 0)

    for k in (1, 7):
        cf[k].wait_recv()
    for k in (0, 2, 6, 8):
        cf[k].start()
    fluid_table(1)
    fluid_table(7)
    cb[3].wait_recv()
    cb[5].wait_recv()
    boulder_table(3)
    boulder_table(5)
    for k in (0, 2, 6, 8):
        cf[k].wait_recv()
        fluid_table(k)

    ones8 = jnp.ones((8, 128), BF16)

    def density(i, _):
        lhs = ut[i][:, 0:48]
        acc = jnp.zeros((128, 128), F32)
        for jj in range(4):
            t2 = jnp.concatenate([tf[fl[0, 0, i, jj * 2]], tf[fl[0, 0, i, jj * 2 + 1]]], axis=1)
            u = jnp.maximum(dot(lhs, jnp.concatenate([t2, t2, t2], axis=0), NN), 0.0)
            sq = u * u
            cube = sq * u
            acc = acc + (cube[:, 0:128] + cube[:, 128:256])
            at = slice(jj * 256, (jj + 1) * 256)
            qh[i, :, at] = sq.astype(BF16)
            ql[i, :, at] = (sq - qh[i, :, at].astype(F32)).astype(BF16)
        a, b = halves(acc)
        total = dot(ones8, a, NT) + dot(ones8, b, NT)
        dens[pl.ds(i, 1), :] = total[0:1]
        return 0

    pack(3)
    pack(5)
    side = gather((3, 5), False)
    beside(0, 8, density, side)
    for k in (1, 7):
        cb[k].wait_recv()
    for k in (0, 2, 6, 8):
        cb[k].start()
    beside(8, 16, density, side)
    rho = fmass[...] + dens[...]
    hd[4] = STIFF * (rho / REST - 1.0) / (rho * rho)
    for k in (1, 7, 3, 5):
        cd[k].start()
    o_fd[...] = jnp.where(f_on, rho, 0.0)

    boulder_table(1)
    boulder_table(7)
    for k in (0, 2, 6, 8):
        cb[k].wait_recv()
        boulder_table(k)

    def coupling(i, _):
        lhs = ut[i][:, 0:48]
        fside = fi[pl.ds(pl.multiple_of(i * 8, 8), 8), :].astype(BF16)
        pulled = jnp.zeros((16, 128), F32)
        for h in range(2):
            n0, n1 = cl[0, 0, i, 2 * h], cl[0, 0, i, 2 * h + 1]
            t2 = jnp.concatenate([tb[n0], tb[n1]], axis=1)
            u = jnp.maximum(dot(lhs, jnp.concatenate([t2, t2, t2], axis=0), NN), 0.0)
            hi, lo = halves(u * u)
            fun = jnp.concatenate([gb[n0], gb[n1]], axis=1)
            pulled = pulled + dot(fun, hi, NT) + dot(fun, lo, NT)
            back = dot(fside, hi, NN) + dot(fside, lo, NN)
            for g in range(2):
                at = pl.ds(pl.multiple_of((i * 4 + 2 * h + g) * 8, 8), 8)
                sp[at, :] = back[:, g * 128 : (g + 1) * 128]
        d4 = pulled[0:4] + pulled[4:8]
        for r in range(4):
            dr[r, pl.ds(i, 1), :] = d4[r : r + 1]
        return 0

    for t in (1, 7, 0, 2, 6, 8):
        pack(t)
    side = gather((1, 7, 0), False)
    beside(0, 10, coupling, side)
    for k in (1, 7):
        cd[k].wait_recv()
    for k in (0, 2, 6, 8):
        cd[k].start()
    beside(10, 16, coupling, side)

    onehot = (
        lax.broadcasted_iota(jnp.int32, (144, 128), 0)
        == jnp.broadcast_to(idc[...].T[0:1], (144, 128))
    ).astype(F32).astype(BF16)

    def reduced(r):
        both = sp[pl.ds(r, 128, stride=8), :] + sp[pl.ds(r + 4, 128, stride=8), :]
        m = jnp.concatenate([v.astype(BF16) for v in split3(both)], axis=1)
        got = dot(onehot, m, NN)
        return got[:, 0:128] + got[:, 128:256] + got[:, 256:384]

    mass_sum = reduced(0)
    for d in range(3):
        pulls = reduced(1 + d)
        for t in range(9):
            at = slice(t * 16, (t + 1) * 16)
            cp[t % 3, t // 3, d] = pulls[at] - hb[t, 4 + d] * mass_sum[at]
    c_yp.start()
    c_ym.start()

    def press_table(t):
        c = hf[t, 0]
        rows = [c] + [c * v for v in centred(hf, t)]
        w = hd[t]
        rows = rows + [w * v for v in rows]
        for r, v in enumerate(rows):
            hi = rounded(v)
            base = t * 512 + r
            stg[pl.ds(base, 32, stride=16), :] = hi
            stg[pl.ds(base + 8, 32, stride=16), :] = v - hi
        settle(ft, t, 32)

    for k in (4, 1, 7):
        press_table(k)
    for k in (3, 5, 0, 2, 6, 8):
        cd[k].wait_recv()
        press_table(k)

    def pressure(i, _):
        fun = jnp.concatenate([ft[fl[0, 0, i, j]] for j in range(8)], axis=1)
        got = dot(fun, qh[i], NT) + dot(fun, ql[i], NT)
        p8 = got[0:8] + got[8:16]
        at = pl.ds(i, 1)
        w_i = hd[4, at, :]
        comb = [w_i * p8[r : r + 1] + p8[4 + r : 5 + r] for r in range(4)]
        for d in range(3):
            pf[d, at, :] = (fpos[d, at, :] - 0.5) * comb[0] - comb[d + 1]
        return 0

    side = gather((2, 6, 8), False)
    beside(0, 8, pressure, side)
    c_yp.wait_recv()
    c_ym.wait_recv()
    for g in range(3):
        red[g] = cp[1, g] + (ry[0, g] + ry[1, g])
    c_xp.start()
    c_xm.start()
    beside(8, 16, pressure, side)
    for d in range(3):
        down = -1.0 if d == 2 else 0.0
        drag = dr[1 + d] - fvel[d] * dr[0]
        o_fa[d] = jnp.where(f_on, PRESS_C * pf[d] + drag + down, 0.0)

    c_xp.wait_recv()
    c_xm.wait_recv()
    for d in range(3):
        o_cp[d] = red[1, d] + (rx[0, d] + rx[1, d])

    for group in (cf, cb, cd):
        for k in group:
            group[k].wait_send()
    for c in (c_yp, c_ym, c_xp, c_xm):
        c.wait_send()


def contact_kernel(
    bcnt, bpos, bvel, brad, bmass, cid, hist, ga, sc, coupled, fa, fd,
    o_fa, o_fd, o_ba, o_h, cnb, pu,
):
    o_fa[...] = fa[...]
    o_fd[...] = fd[...]
    for b in range(16):
        cnb[b : b + 1, :] = jnp.full((1, 128), bcnt[0, 0, b], jnp.int32)
    b_on = lax.broadcasted_iota(jnp.int32, (16, 128), 1) < cnb[...]

    def contact(b, _):
        st = pl.multiple_of(b * 128, 128)
        ids = cid[:, pl.ds(st, 128)]
        tile = ids >> 11
        ox, oy = tile_offsets(tile)
        base = b * 32
        words = [ga[pl.ds(base + w, 8, stride=4), :] for w in range(4)]
        step = sc[0]
        for t in range(1, 9):
            step = jnp.where(tile == t, sc[t], step)
        low = words[3]
        xyz = [
            ((words[d] >> 11) & ((1 << 21) - 1)).astype(F32) * (1.0 / X_UNIT) + 0.5 / X_UNIT
            for d in range(3)
        ]
        pvel = [
            ((((words[d] & 2047) << 5) | ((low >> (10 - 5 * d)) & 31)) - (V_HALF + 1)).astype(F32)
            * step
            for d in range(3)
        ]
        code = (low >> 15) & ((1 << 17) - 1)
        prad = (code - 1).astype(F32) * (1.0 / R_UNIT) + R_LOW
        at = pl.ds(b, 1)
        r1 = row8(bpos[0, at, :]) - (xyz[0] + ox)
        r2 = row8(bpos[1, at, :]) - (xyz[1] + oy)
        r3 = row8(bpos[2, at, :]) - xyz[2]
        dist = jnp.sqrt((r1 * r1 + r2 * r2) + r3 * r3 + SOFT2)
        inv = 1.0 / dist
        nrm = (r1 * inv, r2 * inv, r3 * inv)
        inter = jnp.where(code > 0, jnp.maximum(row8(brad[at, :]) + prad - dist, 0.0), 0.0)
        rel = [row8(bvel[d, at, :]) - pvel[d] for d in range(3)]
        along = (rel[0] * nrm[0] + rel[1] * nrm[1]) + rel[2] * nrm[2]
        touch = jnp.minimum(inter * 100.0, 1.0)
        on = lax.broadcasted_iota(jnp.int32, (8, 128), 1) < jnp.broadcast_to(cnb[at, :], (8, 128))
        for d in range(3):
            spring = (hist[d, :, pl.ds(st, 128)] + DT * (rel[d] - along * nrm[d])) * touch
            push = NORMAL_K * inter * nrm[d] - SHEAR_K * spring
            pu[d, at, :] = jnp.sum(push, axis=0, keepdims=True)
            o_h[d, :, pl.ds(st, 128)] = jnp.where(on, spring, 0.0)
        return 0

    lax.fori_loop(0, 16, contact, 0)

    for d in range(3):
        down = -1.0 if d == 2 else 0.0
        o_ba[d] = jnp.where(b_on, (pu[d] + coupled[d]) / bmass[...] + down, 0.0)


def body(
    fluid_position, fluid_velocity, fluid_mass, fluid_counts, fluid_lists, coupling_lists,
    boulder_position, boulder_velocity, boulder_radius, boulder_mass, boulder_counts,
    contact_ids, spring_history,
):
    n_x, n_y = lax.axis_size("gx"), lax.axis_size("gy")
    vm = pl.BlockSpec(memory_space=pltpu.VMEM)
    sm = pl.BlockSpec(memory_space=pltpu.SMEM)
    pos_b = boulder_position.reshape(3, 16, 128)
    vel_b = boulder_velocity.reshape(3, 16, 128)
    rad_b = boulder_radius.reshape(16, 128)
    mass_b = boulder_mass.reshape(16, 128)
    ids = contact_ids.reshape(8, 2048)
    fa, fd, words, scales, coupled = pl.pallas_call(
        lambda *refs: kernel(*refs, n_x=n_x, n_y=n_y),
        name="step",
        out_shape=(
            jax.ShapeDtypeStruct((3, 32, 128), F32),
            jax.ShapeDtypeStruct((32, 128), F32),
            jax.ShapeDtypeStruct((512, 128), jnp.int32),
            jax.ShapeDtypeStruct((9, 8, 128), F32),
            jax.ShapeDtypeStruct((3, 16, 128), F32),
        ),
        in_specs=[sm] * 4 + [vm] * 8,
        out_specs=(vm,) * 5,
        scratch_shapes=[
            pltpu.VMEM((9, 4, 32, 128), F32),
            pltpu.VMEM((9, 8, 16, 128), F32),
            pltpu.VMEM((9, 32, 128), F32),
            pltpu.VMEM((32, 128, 128), BF16),
            pltpu.VMEM((32, 128, 1024), BF16),
            pltpu.VMEM((32, 128, 1024), BF16),
            pltpu.VMEM((4608, 128), F32),
            pltpu.VMEM((288, 16, 128), BF16),
            pltpu.VMEM((144, 16, 128), BF16),
            pltpu.VMEM((144, 16, 128), BF16),
            pltpu.VMEM((288, 16, 128), BF16),
            pltpu.VMEM((256, 128), F32),
            pltpu.VMEM((1152, 128), jnp.int32),
            pltpu.VMEM((1024, 128), F32),
            pltpu.VMEM((3, 3, 3, 16, 128), F32),
            pltpu.VMEM((2, 3, 3, 16, 128), F32),
            pltpu.VMEM((3, 3, 16, 128), F32),
            pltpu.VMEM((2, 3, 16, 128), F32),
            pltpu.VMEM((128, 128), jnp.int32),
            pltpu.VMEM((32, 128), jnp.int32),
            pltpu.VMEM((16, 128), jnp.int32),
            pltpu.VMEM((32, 128), F32),
            pltpu.VMEM((4, 32, 128), F32),
            pltpu.VMEM((3, 32, 128), F32),
            pltpu.SemaphoreType.DMA((28,)),
            pltpu.SemaphoreType.DMA((28,)),
        ],
        compiler_params=pltpu.CompilerParams(
            collective_id=0, has_side_effects=True, vmem_limit_bytes=67043328
        ),
    )(
        fluid_lists,
        coupling_lists,
        fluid_counts,
        boulder_counts,
        fluid_position.reshape(3, 32, 128),
        fluid_velocity.reshape(3, 32, 128),
        fluid_mass.reshape(32, 128),
        pos_b,
        vel_b,
        rad_b,
        mass_b,
        ids,
    )
    fa, fd, ba, ho = pl.pallas_call(
        contact_kernel,
        name="contact",
        out_shape=(
            jax.ShapeDtypeStruct((3, 32, 128), F32),
            jax.ShapeDtypeStruct((32, 128), F32),
            jax.ShapeDtypeStruct((3, 16, 128), F32),
            jax.ShapeDtypeStruct((3, 8, 2048), F32),
        ),
        in_specs=[sm] + [vm] * 11,
        out_specs=(vm,) * 4,
        scratch_shapes=[pltpu.VMEM((16, 128), jnp.int32), pltpu.VMEM((3, 16, 128), F32)],
        compiler_params=pltpu.CompilerParams(vmem_limit_bytes=67043328),
    )(
        boulder_counts, pos_b, vel_b, rad_b, mass_b, ids,
        spring_history.reshape(3, 8, 2048), words, scales, coupled, fa, fd,
    )
    return (
        fa.reshape(3, 1, 1, 4096),
        fd.reshape(1, 1, 4096),
        ba.reshape(3, 1, 1, 2048),
        ho.reshape(3, 1, 1, 8, 2048),
    )


def solution(mesh):
    v4 = P(None, "gx", "gy", None)
    v3 = P("gx", "gy", None)
    l4 = P("gx", "gy", None, None)
    h5 = P(None, "gx", "gy", None, None)
    return jax.shard_map(
        body,
        mesh=mesh,
        in_specs=(v4, v4, v3, v3, l4, l4, v4, v4, v3, v3, v3, l4, h5),
        out_specs=(v4, v3, v4, h5),
        check_vma=False,
    )
```
